512 devices in a mesh: tp: 64 (over y, z_hi, core), ep: 8 (over x, z_lo).
Axes of the slice: x: 4, y: 8, z: 8 (z_hi: 4, z_lo: 2; z = z_hi * 2 + z_lo), core: 2. Of those that a mesh axis runs over, the one named last changes fastest.
Arguments:
- residual: bfloat16 [8, 7168, 256], P('ep', 'tp')
- out_grad: bfloat16 [8, 7168, 256], P('ep', 'tp'), may hold values from -6 to 6
- norm_gain: float32 [7168], P('tp'), may hold values from 0.25 to 1.75
- context: bfloat16 [8, 16384, 256], P('ep', 'tp'), may hold values from -0.3125 to 0.3125
- w_out: bfloat16 [7168, 16384], P('ep', 'tp'), may hold values from -0.046875 to 0.046875
- w_gate: bfloat16 [8, 7168, 2048], P('ep', 'tp'), may hold values from -0.0625 to 0.0625
- w_up: bfloat16 [8, 7168, 2048], P('ep', 'tp'), may hold values from -0.0625 to 0.0625
- w_down: bfloat16 [8, 7168, 2048], P('ep', 'tp'), may hold values from -0.125 to 0.125
- slot_token: int32 [8, 8, 8], P('ep'), may hold values from 0 to 255, as said below
- slot_count: int32 [8, 8], P('ep'), may hold values from 1 to 8, as said below
- slot_gate: float32 [8, 8, 8], P('ep'), may hold values from 0.25 to 2.5
Outputs:
- resid_grad: bfloat16 [8, 7168, 256], P('ep', 'tp')
- context_grad: bfloat16 [8, 16384, 256], P('ep', 'tp')
- w_out_grad: bfloat16 [7168, 16384], P('ep', 'tp')
- gate_grad: bfloat16 [8, 7168, 2048], P('ep', 'tp')
- up_grad: bfloat16 [8, 7168, 2048], P('ep', 'tp')
- down_grad: bfloat16 [8, 7168, 2048], P('ep', 'tp')
The draws below stay inside these ranges and needn't reach their ends.
Inputs may be any that keep to these rules, and one draw needn't show every extreme that they name: `slot_token`: within one group and expert the 8 token positions are distinct; slots at or beyond slot_count are unused. `slot_count`: in every draw one expert has 8 tokens from every group.
All inputs are finite; a program needn't handle non-finite values.
Results may differ from the reference program's by a relative error of at most 0.014.
Values may be sent and summed in bfloat16 or wider, within the bound.
A program may use at most 64 MiB of HBM per device.

```python
import math
import jax
import jax.numpy as jnp
from jax import lax

D = 7168
EXP_HIDDEN = 2048
GROUP = 256
CAP = 8
ATT = 16384
GROUPS = 8
EXPERTS = 8


def draw_residual(key, part):
    feature_idx = jnp.arange(D, dtype=jnp.float32) / max(D - 1, 1)
    rising = 20.0 ** feature_idx
    noise = jnp.clip(jax.random.normal(jax.random.fold_in(key, 31), (GROUPS, D, GROUP), jnp.float32), -4.0, 4.0)
    token_scale = jnp.exp(jax.random.uniform(jax.random.fold_in(key, 32), (GROUPS, 1, GROUP), jnp.float32, 0.0, 1.6))
    return (0.3 * noise * rising[None, :, None] * token_scale).astype(jnp.bfloat16)


def draw_slot_token(key, part):
    subkeys = jax.random.split(jax.random.fold_in(key, 11), GROUPS * EXPERTS)
    orders = jax.vmap(lambda sub: jax.random.permutation(sub, GROUP))(subkeys)
    return orders[:, :CAP].reshape(GROUPS, EXPERTS, CAP).astype(jnp.int32)


def draw_slot_count(key, part):
    baseline = jax.random.randint(jax.random.fold_in(key, 21), (GROUPS, EXPERTS), 1, CAP // 2 + 1)
    busiest = jax.random.randint(jax.random.fold_in(key, 22), (), 0, EXPERTS)
    chosen = jnp.arange(EXPERTS)[None, :] == busiest
    return jnp.where(chosen, CAP, baseline).astype(jnp.int32)


def block_levels(key, dims, cuts, least, largest):
    def one(dim, shards_of):
        draws = jax.random.uniform(jax.random.fold_in(jax.random.fold_in(key, 6), dim), (shards_of,), jnp.float32, least / len(cuts), largest / len(cuts))
        return jnp.repeat(jnp.exp(draws), dims[dim] // shards_of).reshape((-1,) + (1,) * (len(dims) - dim - 1))

    level = one(*cuts[0])
    for cut in cuts[1:]:
        level = level * one(*cut)
    return level


def bell_draw(key, extent, scale, limit, pieces=(), held_as=jnp.bfloat16):
    array = jax.random.normal(key, extent, jnp.float32) * scale
    if len(pieces) > 0:
        array = block_levels(key, extent, pieces, -0.22, 0.18) * array
    return jnp.clip(array, min=-limit, max=limit).astype(held_as)


def setup_inputs(seed: int = 0) -> dict:
    keys = jax.random.split(jax.random.key(seed), 12)
    return {
        "residual": draw_residual(jax.random.fold_in(keys[11], 71), 0),
        "out_grad": bell_draw(keys[1], (GROUPS, D, GROUP), 1.0, 6.0, ((0, 8), (1, 64))),
        "norm_gain": jnp.clip(1.0 + 0.15 * jax.random.normal(keys[2], (D,), jnp.float32), 0.25, 1.75),
        "context": bell_draw(keys[3], (GROUPS, ATT, GROUP), ((GROUPS * GROUP) ** -0.5), 0.3125, ((0, 8), (1, 64))),
        "w_out": bell_draw(keys[4], (D, ATT), ATT ** -0.5, 0.046875, ((0, 8), (1, 64))),
        "w_gate": bell_draw(keys[5], (EXPERTS, D, EXP_HIDDEN), D ** -0.5, 0.0625, ((0, 8), (1, 64))),
        "w_up": bell_draw(keys[6], (EXPERTS, D, EXP_HIDDEN), D ** -0.5, 0.0625, ((0, 8), (1, 64))),
        "w_down": bell_draw(keys[7], (EXPERTS, D, EXP_HIDDEN), EXP_HIDDEN ** -0.5, 0.125, ((0, 8), (1, 64))),
        "slot_token": draw_slot_token(jax.random.fold_in(keys[11], 71), 0),
        "slot_count": draw_slot_count(jax.random.fold_in(keys[11], 71), 0),
        "slot_gate": jnp.clip(jnp.exp(math.log(2.5) - 2.3025851 * jax.random.uniform(keys[10], (GROUPS, EXPERTS, CAP), jnp.float32) ** block_levels(keys[10], (GROUPS, EXPERTS, CAP), ((0, 8),), -0.2, 0.2)), 0.25, 2.5),
    }


norm_eps = 1e-06

def expert_backward(operands):
    rows_x, rows_go, gate_w, up_w, down_w = operands
    pre_gate = jnp.dot(rows_x, gate_w, preferred_element_type=jnp.float32)
    pre_up = jnp.dot(rows_x, up_w, preferred_element_type=jnp.float32)
    hid_grad = jnp.dot(rows_go, down_w, preferred_element_type=jnp.float32)
    sigmoid_gate = jax.nn.sigmoid(pre_gate)
    silu_gate = pre_gate * sigmoid_gate
    hidden = (silu_gate * pre_up).astype(jnp.bfloat16)
    d_gate = (hid_grad * pre_up * sigmoid_gate * (1.0 + pre_gate * (1.0 - sigmoid_gate))).astype(jnp.bfloat16)
    d_up = (hid_grad * silu_gate).astype(jnp.bfloat16)
    down_grad = jnp.dot(rows_go.T, hidden, preferred_element_type=jnp.float32).astype(jnp.bfloat16)
    gate_grad = jnp.dot(rows_x.T, d_gate, preferred_element_type=jnp.float32).astype(jnp.bfloat16)
    up_grad = jnp.dot(rows_x.T, d_up, preferred_element_type=jnp.float32).astype(jnp.bfloat16)
    slot_back = (jnp.dot(d_gate, gate_w.T, preferred_element_type=jnp.float32) + jnp.dot(d_up, up_w.T, preferred_element_type=jnp.float32)).astype(jnp.bfloat16)
    return (slot_back, gate_grad, up_grad, down_grad)

def pick_rows(source, slot_table):
    return source[slot_table]

def add_rows(slot_table, values):
    summed = jnp.zeros((GROUP, D), jnp.float32)
    return summed.at[slot_table.reshape(-1)].add(values.reshape(-1, D).astype(jnp.float32))

def reference(residual, out_grad, norm_gain, context, w_out, w_gate, w_up, w_down, slot_token, slot_count, slot_gate):
    stream = residual.astype(jnp.float32).transpose(0, 2, 1)
    inv_rms = lax.rsqrt(lax.optimization_barrier(jnp.mean(stream * stream, axis=-1, keepdims=True)) + norm_eps)
    normed = stream * inv_rms
    inputs = (normed * norm_gain).astype(jnp.bfloat16)
    grad_in = out_grad.astype(jnp.float32).transpose(0, 2, 1)
    live_mask = (jnp.arange(CAP)[None, None, :] < slot_count[:, :, None])[..., None]
    slot_in = jnp.where(live_mask, jax.vmap(pick_rows)(inputs, slot_token), jnp.zeros((), jnp.bfloat16))
    slot_go = jnp.where(live_mask, slot_gate[..., None] * jax.vmap(pick_rows)(grad_in, slot_token), 0.0).astype(jnp.bfloat16)
    rows_x = slot_in.transpose(1, 0, 2, 3).reshape(EXPERTS, GROUPS * CAP, D)
    rows_go = slot_go.transpose(1, 0, 2, 3).reshape(EXPERTS, GROUPS * CAP, D)
    slot_back, gate_grad, up_grad, down_grad = lax.map(expert_backward, (rows_x, rows_go, w_gate, w_up, w_down))
    slot_back = slot_back.reshape(EXPERTS, GROUPS, CAP, D).transpose(1, 0, 2, 3)
    in_grad = jax.vmap(add_rows)(slot_token, slot_back).astype(jnp.bfloat16)
    scaled = in_grad.astype(jnp.float32) * norm_gain
    center = lax.optimization_barrier(jnp.mean(scaled * normed, axis=-1, keepdims=True))
    resid_tok = (grad_in + inv_rms * (scaled - normed * center)).astype(jnp.bfloat16)
    context_grad = lax.map(lambda grad_rows: jnp.dot(grad_rows, w_out, preferred_element_type=jnp.float32).astype(jnp.bfloat16).T, resid_tok)
    context_tok = context.transpose(0, 2, 1).reshape(GROUPS * GROUP, ATT)
    w_out_grad = jnp.dot(resid_tok.reshape(GROUPS * GROUP, D).T, context_tok, preferred_element_type=jnp.float32).astype(jnp.bfloat16)
    resid_grad = resid_tok.transpose(0, 2, 1)
    return (resid_grad, context_grad, w_out_grad, gate_grad, up_grad, down_grad)
```

```python
import functools

import jax
import jax.numpy as jnp
from jax import lax
from jax.experimental import pallas as pl
from jax.experimental.pallas import tpu as pltpu
from jax.sharding import PartitionSpec as P

norm_eps = 1e-06
MESH = pl.DeviceIdType.MESH
BF = jnp.bfloat16
F32 = jnp.float32


def mm(left, right):
    return lax.dot_general(
        left, right, (((1,), (0,)), ((), ())), preferred_element_type=F32
    )


def mm_nt(left, right):
    return lax.dot_general(
        left, right, (((1,), (1,)), ((), ())), preferred_element_type=F32
    )


def mm_tn(left, right):
    return lax.dot_general(
        left, right, (((0,), (0,)), ((), ())), preferred_element_type=F32
    )


def eye_mask(n):
    rows = lax.broadcasted_iota(jnp.int32, (n, n), 0)
    cols = lax.broadcasted_iota(jnp.int32, (n, n), 1)
    return rows == cols


def col_to_row(col):
    n = col.shape[0]
    return jnp.sum(
        jnp.where(eye_mask(n), jnp.broadcast_to(col, (n, n)), 0.0), axis=0, keepdims=True
    )


def row_to_col(row):
    n = row.shape[1]
    return jnp.sum(
        jnp.where(eye_mask(n), jnp.broadcast_to(row, (n, n)), 0.0), axis=1, keepdims=True
    )


def kernel(
    dims,
    res_ref,
    og_ref,
    gain_ref,
    ctx_ref,
    wo_ref,
    wg_ref,
    wu_ref,
    wd_ref,
    tok_send_x,
    tok_send_go,
    send_scale,
    tok_slot,
    resid_out,
    ctx_out,
    wo_out,
    gate_out,
    up_out,
    down_out,
    a_send,
    a_recv,
    og_all,
    ctx_all,
    sel_all,
    sel_perm,
    part_out,
    part_own,
    core_recv,
    part1,
    y_recv,
    part2,
    z_recv,
    tile_sq,
    tile_sq_c,
    tile_sq_y,
    tile_sq_z,
    tile_dot,
    tile_dot_c,
    tile_dot_y,
    tile_dot_z,
    inv_buf,
    dot_buf,
    act,
    ret_send,
    ret_recv,
    delta_own,
    delta_all,
    base_send,
    base_recv,
    wo_acc,
    msg_send,
    msg_recv,
    sem_a,
    sem_ogt,
    sem_oga,
    sem_ogb,
    sem_ogk,
    sem_ctx,
    sem_sel,
    sem_core,
    sem_y,
    sem_z,
    sem_sqc,
    sem_sqy,
    sem_sqz,
    sem_dtc,
    sem_dty,
    sem_dtz,
    sem_actz,
    sem_acty,
    sem_actk,
    sem_ret,
    sem_dt,
    sem_da,
    sem_db,
    sem_dk,
    sem_base,
    sem_msg,
):
    NE, NY, NZ, CAP, FS, T, A, H, D = dims
    S = NE * CAP
    SZ = S // NZ
    HC = H // 2
    HY = HC // NY
    TH = T // 2
    SH = S // 2

    ep = lax.axis_index("ep")
    tp = lax.axis_index("tp")
    y = tp // (NZ * 2)
    c = tp % (NZ * 2)
    z = c // 2
    k = c % 2

    def tp_of(yy, zz, kk):
        return (yy * NZ + zz) * 2 + kk

    def ep_dev(i):
        return {"ep": (ep + i) % NE, "tp": tp}

    def y_dev(i):
        return {"ep": ep, "tp": tp_of((y + i) % NY, z, k)}

    def z_dev(i):
        return {"ep": ep, "tp": tp_of(y, (z + i) % NZ, k)}

    sib = {"ep": ep, "tp": tp_of(y, z, 1 - k)}
    cross = {"ep": y, "tp": tp_of(ep, z, k)}
    diag = ep == y

    def remote(src, dst, sems, i, dev):
        return pltpu.make_async_remote_copy(
            src_ref=src,
            dst_ref=dst,
            send_sem=sems.at[0, i],
            recv_sem=sems.at[1, i],
            device_id=dev,
            device_id_type=MESH,
        )

    started = []

    def go(copies):
        for one in copies:
            one.start()
        started.extend(copies)
        return copies

    def arrive(copies):
        for one in copies:
            one.wait_recv()

    barrier = pltpu.get_barrier_semaphore()
    for i in range(1, NE):
        pl.semaphore_signal(barrier, inc=1, device_id=ep_dev(i), device_id_type=MESH)
    for i in range(1, NY):
        pl.semaphore_signal(barrier, inc=1, device_id=y_dev(i), device_id_type=MESH)
    for i in range(1, NZ):
        pl.semaphore_signal(barrier, inc=1, device_id=z_dev(i), device_id_type=MESH)
    pl.semaphore_signal(barrier, inc=1, device_id=sib, device_id_type=MESH)

    @pl.when(jnp.logical_not(diag))
    def _():
        pl.semaphore_signal(barrier, inc=1, device_id=cross, device_id_type=MESH)

    def one_hot(tokens_ref, rows):
        lanes = lax.broadcasted_iota(jnp.int32, (rows, T), 1)
        return jnp.where(tokens_ref[...] == lanes, 1.0, 0.0).astype(BF)

    picked = mm_nt(one_hot(tok_send_x, 2 * S), res_ref[...]) + mm_nt(
        one_hot(tok_send_go, 2 * S), og_ref[...]
    )
    a_send[...] = (send_scale[...] * picked).astype(BF).reshape(NE, 2 * CAP, FS)

    peers = NE - 1 + NY - 1 + NZ
    pl.semaphore_wait(barrier, jnp.where(diag, peers, peers + 1))

    a_copies = go(
        [
            remote(a_send.at[(ep + i) % NE], a_recv.at[ep], sem_a, i, ep_dev(i))
            for i in range(1, NE)
        ]
    )
    og_cross = remote(og_ref, og_all.at[ep, z, k], sem_ogt, 0, cross)

    @pl.when(jnp.logical_not(diag))
    def _():
        og_cross.start()

    @pl.when(diag)
    def _():
        og_all[ep, z, k] = og_ref[...]

    a_recv[ep] = a_send[ep]
    ctx_copies = go(
        [remote(ctx_ref, ctx_all.at[ep], sem_ctx, i, ep_dev(i)) for i in range(1, NE)]
    )
    oh_slot = one_hot(tok_slot, S)
    sel_all[ep] = mm_nt(oh_slot, ctx_ref[...]).astype(BF)
    sel_copies = go(
        [remote(sel_all.at[ep], sel_all.at[ep], sem_sel, i, ep_dev(i)) for i in range(1, NE)]
    )
    ctx_all[ep] = ctx_ref[...]

    arrive(a_copies)
    rows = a_recv[...].astype(F32).reshape(NE, 2, CAP, FS)
    rows_x = rows[:, 0].reshape(S, FS)
    rows_go = rows[:, 1].reshape(S, FS)
    rows_xg = (rows_x * gain_ref[...]).astype(BF)
    rows_gob = rows_go.astype(BF)
    other = pl.ds(pl.multiple_of((1 - k) * HC, HC), HC)
    own = pl.ds(pl.multiple_of(k * HC, HC), HC)
    lefts = (rows_xg, rows_xg, rows_gob)
    weights = (wg_ref, wu_ref, wd_ref)
    for n in range(3):
        part_out[n] = mm(lefts[n], weights[n][:, other]).astype(BF)
    core_copies = go([remote(part_out, core_recv, sem_core, 0, sib)])
    sq_row = col_to_row(jnp.sum(rows_x * rows_x, axis=1, keepdims=True))
    tile_sq[0] = jnp.broadcast_to(sq_row, (8, S))
    sqc = go([remote(tile_sq.at[0], tile_sq_c, sem_sqc, 0, sib)])

    @pl.when(jnp.logical_not(diag))
    def _():
        og_cross.wait_recv()

    oga1 = go(
        [
            remote(
                og_all.at[y, z, k, :, pl.ds(0, TH)],
                og_all.at[y, z, k, :, pl.ds(0, TH)],
                sem_oga,
                i,
                y_dev(i),
            )
            for i in range(1, NY)
        ]
    )
    ogb1 = go(
        [
            remote(
                og_all.at[y, z, k, :, pl.ds(TH, TH)],
                og_all.at[y, z, k, :, pl.ds(TH, TH)],
                sem_ogb,
                i,
                z_dev(i),
            )
            for i in range(1, NZ)
        ]
    )

    for n in range(3):
        part_own[n] = mm(lefts[n], weights[n][:, own])

    arrive(core_copies)
    part1[...] = (part_own[...] + core_recv[...].astype(F32)).astype(BF)

    def y_cols(i):
        return pl.ds(pl.multiple_of(((y + i) % NY) * HY, HY), HY)

    y_copies = go(
        [
            remote(part1.at[:, :, y_cols(i)], y_recv.at[i - 1], sem_y, i, y_dev(i))
            for i in range(1, NY)
        ]
    )
    arrive(sqc)
    tile_sq[1] = tile_sq[0] + tile_sq_c[...]
    sqy = go(
        [remote(tile_sq.at[1], tile_sq_y.at[i - 1], sem_sqy, i, y_dev(i)) for i in range(1, NY)]
    )
    arrive(y_copies)
    total = part1[:, :, y_cols(0)].astype(F32)
    for i in range(1, NY):
        total = total + y_recv[i - 1].astype(F32)
    part2[...] = total.astype(BF)

    def z_rows(i):
        return pl.ds(pl.multiple_of(((z + i) % NZ) * SZ, SZ), SZ)

    z_copies = go(
        [
            remote(part2.at[:, z_rows(i), :], z_recv.at[i - 1], sem_z, i, z_dev(i))
            for i in range(1, NZ)
        ]
    )
    arrive(sqy)
    sq = tile_sq[1]
    for i in range(1, NY):
        sq = sq + tile_sq_y[i - 1]
    tile_sq[2] = sq
    sqz = go(
        [remote(tile_sq.at[2], tile_sq_z.at[i - 1], sem_sqz, i, z_dev(i)) for i in range(1, NZ)]
    )
    arrive(sqz)
    sq = tile_sq[2]
    for i in range(1, NZ):
        sq = sq + tile_sq_z[i - 1]
    inv_col = row_to_col(lax.rsqrt(sq[0:1] / D + norm_eps))
    inv_buf[...] = jnp.broadcast_to(inv_col, (S, 128))
    arrive(z_copies)
    total = part2[:, z_rows(0), :].astype(F32)
    for i in range(1, NZ):
        total = total + z_recv[i - 1].astype(F32)
    inv_mine = inv_buf[z_rows(0), 0:HY] if HY <= 128 else inv_buf[z_rows(0), 0:1]
    pre_gate = inv_mine * total[0]
    pre_up = inv_mine * total[1]
    hid_grad = total[2]
    sigmoid_gate = jax.nn.sigmoid(pre_gate)
    silu_gate = pre_gate * sigmoid_gate
    hidden = (silu_gate * pre_up).astype(BF)
    d_gate = (hid_grad * pre_up * sigmoid_gate * (1.0 + pre_gate * (1.0 - sigmoid_gate))).astype(BF)
    d_up = (hid_grad * silu_gate).astype(BF)
    my_cols = pl.ds(pl.multiple_of(k * HC + y * HY, HY), HY)
    act[0, z_rows(0), my_cols] = d_gate
    act[1, z_rows(0), my_cols] = d_up
    act[2, z_rows(0), my_cols] = hidden

    mine = act.at[:, z_rows(0), my_cols]
    actz = go([remote(mine, mine, sem_actz, i, z_dev(i)) for i in range(1, NZ)])
    dots = jnp.sum(d_gate.astype(F32) * pre_gate + d_up.astype(F32) * pre_up, axis=1, keepdims=True)
    dot_buf[...] = jnp.zeros_like(dot_buf)
    dot_buf[z_rows(0), :] = jnp.broadcast_to(dots, (SZ, 128))
    tile_dot[0] = jnp.broadcast_to(col_to_row(dot_buf[:, 0:1]), (8, S))
    dtz = go(
        [remote(tile_dot.at[0], tile_dot_z.at[i - 1], sem_dtz, i, z_dev(i)) for i in range(1, NZ)]
    )
    arrive(actz)
    mine_y = act.at[:, :, my_cols]
    acty = go([remote(mine_y, mine_y, sem_acty, i, y_dev(i)) for i in range(1, NY)])
    arrive(dtz)
    dt = tile_dot[0]
    for i in range(1, NZ):
        dt = dt + tile_dot_z[i - 1]
    tile_dot[1] = dt
    dty = go(
        [remote(tile_dot.at[1], tile_dot_y.at[i - 1], sem_dty, i, y_dev(i)) for i in range(1, NY)]
    )

    arrive(oga1)
    oga2 = go(
        [
            remote(
                og_all.at[:, z, k, :, pl.ds(0, TH)],
                og_all.at[:, z, k, :, pl.ds(0, TH)],
                sem_oga,
                NY + i,
                z_dev(i),
            )
            for i in range(1, NZ)
        ]
    )
    arrive(ogb1)
    ogb2 = go(
        [
            remote(
                og_all.at[y, :, k, :, pl.ds(TH, TH)],
                og_all.at[y, :, k, :, pl.ds(TH, TH)],
                sem_ogb,
                NZ + i,
                y_dev(i),
            )
            for i in range(1, NY)
        ]
    )

    arrive(acty)
    mine_k = act.at[:, :, own]
    actk = go([remote(mine_k, mine_k, sem_actk, 0, sib)])
    arrive(dty)
    dt = tile_dot[1]
    for i in range(1, NY):
        dt = dt + tile_dot_y[i - 1]
    tile_dot[2] = dt
    dtc = go([remote(tile_dot.at[2], tile_dot_c, sem_dtc, 0, sib)])
    arrive(dtc)
    dots_col = row_to_col((tile_dot[2] + tile_dot_c[...])[0:1])
    inv_col = inv_buf[:, 0:1]
    normed = rows_x * inv_col
    arrive(actk)
    slot_back = (
        (mm_nt(act[0], wg_ref[...]) + mm_nt(act[1], wu_ref[...])).astype(BF).astype(F32)
    )
    delta = inv_col * (gain_ref[...] * slot_back - normed * (dots_col / D))
    delta_own[...] = delta.astype(BF)

    d_cross = remote(delta_own, delta_all.at[z, k, ep], sem_dt, 0, cross)

    @pl.when(jnp.logical_not(diag))
    def _():
        d_cross.start()

    @pl.when(diag)
    def _():
        delta_all[z, k, ep] = delta_own[...]

    ret_send[...] = delta.reshape(NE, CAP, FS)
    ret_recv[ep] = ret_send[ep]
    ret_copies = go(
        [
            remote(ret_send.at[(ep + i) % NE], ret_recv.at[ep], sem_ret, i, ep_dev(i))
            for i in range(1, NE)
        ]
    )

    slot_in = (normed * gain_ref[...]).astype(BF)
    gate_out[...] = mm_tn(slot_in, act[0]).astype(BF)

    @pl.when(jnp.logical_not(diag))
    def _():
        d_cross.wait_recv()

    da = delta_all.at[z, k, y, pl.ds(0, SH)]
    db = delta_all.at[z, k, y, pl.ds(SH, SH)]
    da1 = go([remote(da, da, sem_da, i, y_dev(i)) for i in range(1, NY)])
    db1 = go([remote(db, db, sem_db, i, z_dev(i)) for i in range(1, NZ)])
    up_out[...] = mm_tn(slot_in, act[1]).astype(BF)
    down_out[...] = mm_tn(rows_gob, act[2]).astype(BF)
    arrive(db1)
    db = delta_all.at[:, k, y, pl.ds(SH, SH)]
    db2 = go([remote(db, db, sem_db, NZ + i, y_dev(i)) for i in range(1, NY)])
    arrive(da1)
    da = delta_all.at[z, k, :, pl.ds(0, SH)]
    da2 = go([remote(da, da, sem_da, NY + i, z_dev(i)) for i in range(1, NZ)])

    arrive(ogb2)
    arrive(oga2)
    ogk_mine = og_all.at[:, :, k]
    ogk = go([remote(ogk_mine, ogk_mine, sem_ogk, 0, sib)])
    arrive(sel_copies)
    sel = sel_all[...].astype(F32).reshape(NE, NE, CAP, A)
    for e in range(NE):
        sel_perm[e] = sel[:, e].reshape(S, A).astype(BF)
    arrive(ctx_copies)
    arrive(da2)
    arrive(db2)
    dk_mine = delta_all.at[:, k]
    dk = go([remote(dk_mine, dk_mine, sem_dk, 0, sib)])
    arrive(ogk)
    BL = NZ * 2 * FS
    for g in range(NE):
        block = og_all[g].reshape(BL, T)
        base_send[g] = mm_tn(wo_ref[...], block).astype(BF)
        one = mm_nt(block, ctx_all[g])
        if g == 0:
            wo_acc[...] = one
        else:
            wo_acc[...] += one
    base_recv[ep] = base_send[ep]
    base_copies = go(
        [
            remote(base_send.at[(ep + i) % NE], base_recv.at[ep], sem_base, i, ep_dev(i))
            for i in range(1, NE)
        ]
    )

    arrive(dk)
    slots = None
    for q in range(NZ * 2):
        feats = pl.ds(q * FS, FS)
        block = delta_all[q // 2, q % 2].reshape(NE * S, FS)
        one = mm(block, wo_ref[feats, :])
        slots = one if slots is None else slots + one
    slots = slots.reshape(NE, NE, CAP, A)
    for g in range(NE):
        msg_send[g] = slots[:, g].reshape(S, A).astype(BF)
    msg_recv[ep] = msg_send[ep]
    msg_copies = go(
        [
            remote(msg_send.at[(ep + i) % NE], msg_recv.at[ep], sem_msg, i, ep_dev(i))
            for i in range(1, NE)
        ]
    )
    right = sel_perm[...].reshape(NE * S, A)
    for q in range(NZ * 2):
        feats = pl.ds(q * FS, FS)
        block = delta_all[q // 2, q % 2].reshape(NE * S, FS)
        wo_out[feats, :] = (wo_acc[feats, :] + mm_tn(block, right)).astype(BF)

    arrive(ret_copies)
    returned = ret_recv[...].reshape(S, FS).astype(BF)
    resid_out[...] = (og_ref[...].astype(F32) + mm_tn(returned, oh_slot)).astype(BF)

    arrive(base_copies)
    total = base_recv[0].astype(F32)
    for i in range(1, NE):
        total = total + base_recv[i].astype(F32)
    arrive(msg_copies)
    picked = msg_recv[0].astype(F32)
    for i in range(1, NE):
        picked = picked + msg_recv[i].astype(F32)
    ctx_out[...] = (total + mm_tn(picked.astype(BF), oh_slot)).astype(BF)

    for one in started:
        one.wait_send()

    @pl.when(jnp.logical_not(diag))
    def _():
        og_cross.wait_send()
        d_cross.wait_send()


def shards(
    dims,
    residual,
    out_grad,
    norm_gain,
    context,
    w_out,
    w_gate,
    w_up,
    w_down,
    slot_token,
    slot_count,
    slot_gate,
):
    NE, NY, NZ, CAP, FS, T, A, H, D = dims
    S = NE * CAP
    BL = NZ * 2 * FS
    table = slot_token[0]
    live = jnp.arange(CAP)[None, :] < slot_count[0][:, None]
    table = jnp.where(live, table, -1)
    none = jnp.full_like(table, -1)
    tok_x = jnp.stack([table, none], axis=1).reshape(2 * S, 1)
    tok_go = jnp.stack([none, table], axis=1).reshape(2 * S, 1)
    scale = jnp.stack([jnp.ones_like(slot_gate[0]), slot_gate[0]], axis=1).reshape(2 * S, 1)
    tok_slot = table.reshape(S, 1)
    HC = H // 2
    HY = HC // NY
    SZ = S // NZ
    V = pltpu.VMEM
    dma = pltpu.SemaphoreType.DMA
    whole = pl.BlockSpec(memory_space=pltpu.VMEM)
    out_shape = (
        jax.ShapeDtypeStruct((FS, T), BF),
        jax.ShapeDtypeStruct((A, T), BF),
        jax.ShapeDtypeStruct((BL, A), BF),
        jax.ShapeDtypeStruct((FS, H), BF),
        jax.ShapeDtypeStruct((FS, H), BF),
        jax.ShapeDtypeStruct((FS, H), BF),
    )
    scratch = [
        V((NE, 2 * CAP, FS), BF),
        V((NE, 2 * CAP, FS), BF),
        V((NE, NZ, 2, FS, T), BF),
        V((NE, A, T), BF),
        V((NE, S, A), BF),
        V((NE, S, A), BF),
        V((3, S, HC), BF),
        V((3, S, HC), F32),
        V((3, S, HC), BF),
        V((3, S, HC), BF),
        V((NY - 1, 3, S, HY), BF),
        V((3, S, HY), BF),
        V((NZ - 1, 3, SZ, HY), BF),
        V((3, 8, S), F32),
        V((8, S), F32),
        V((NY - 1, 8, S), F32),
        V((NZ - 1, 8, S), F32),
        V((3, 8, S), F32),
        V((8, S), F32),
        V((NY - 1, 8, S), F32),
        V((NZ - 1, 8, S), F32),
        V((S, 128), F32),
        V((S, 128), F32),
        V((3, S, H), BF),
        V((NE, CAP, FS), F32),
        V((NE, CAP, FS), F32),
        V((S, FS), BF),
        V((NZ, 2, NE, S, FS), BF),
        V((NE, A, T), BF),
        V((NE, A, T), BF),
        V((BL, A), F32),
        V((NE, S, A), BF),
        V((NE, S, A), BF),
        dma((2, NE)),
        dma((2, 1)),
        dma((2, NY + NZ)),
        dma((2, NY + NZ)),
        dma((2, 1)),
        dma((2, NE)),
        dma((2, NE)),
        dma((2, 1)),
        dma((2, NY)),
        dma((2, NZ)),
        dma((2, 1)),
        dma((2, NY)),
        dma((2, NZ)),
        dma((2, 1)),
        dma((2, NY)),
        dma((2, NZ)),
        dma((2, NZ)),
        dma((2, NY)),
        dma((2, 1)),
        dma((2, NE)),
        dma((2, 1)),
        dma((2, NY + NZ)),
        dma((2, NY + NZ)),
        dma((2, 1)),
        dma((2, NE)),
        dma((2, NE)),
    ]
    resid, ctx_grad, wo_grad, gate_grad, up_grad, down_grad = pl.pallas_call(
        functools.partial(kernel, dims),
        out_shape=out_shape,
        in_specs=[whole] * 12,
        out_specs=[whole] * 6,
        scratch_shapes=scratch,
        compiler_params=pltpu.CompilerParams(
            collective_id=0, has_side_effects=True, vmem_limit_bytes=48 * 1024 * 1024
        ),
    )(
        residual[0],
        out_grad[0],
        norm_gain.reshape(1, FS),
        context[0],
        w_out,
        w_gate[0],
        w_up[0],
        w_down[0],
        tok_x,
        tok_go,
        scale,
        tok_slot,
    )
    return (
        resid[None],
        ctx_grad[None],
        wo_grad,
        gate_grad[None],
        up_grad[None],
        down_grad[None],
    )


def solution(mesh):
    sizes = dict(mesh.shape)
    NE = sizes["ep"]
    NY = NE
    NZ = sizes["tp"] // (2 * NY)

    def run(residual, out_grad, norm_gain, context, w_out, w_gate, w_up, w_down, *slots):
        D, T = residual.shape[1:]
        dims = (
            NE,
            NY,
            NZ,
            slots[0].shape[2],
            D // sizes["tp"],
            T,
            context.shape[1] // sizes["tp"],
            w_gate.shape[2],
            D,
        )
        return jax.shard_map(
            functools.partial(shards, dims),
            mesh=mesh,
            in_specs=(
                P("ep", "tp", None),
                P("ep", "tp", None),
                P("tp"),
                P("ep", "tp", None),
                P("ep", "tp"),
                P("ep", "tp", None),
                P("ep", "tp", None),
                P("ep", "tp", None),
                P("ep", None, None),
                P("ep", None),
                P("ep", None, None),
            ),
            out_specs=(
                P("ep", "tp", None),
                P("ep", "tp", None),
                P("ep", "tp"),
                P("ep", "tp", None),
                P("ep", "tp", None),
                P("ep", "tp", None),
            ),
            check_vma=False,
        )(residual, out_grad, norm_gain, context, w_out, w_gate, w_up, w_down, *slots)

    return run
```

```python
import functools

import jax
import jax.numpy as jnp
from jax import lax
from jax.experimental import pallas as pl
from jax.experimental.pallas import tpu as pltpu
from jax.sharding import PartitionSpec as P

norm_eps = 1e-06
MESH = pl.DeviceIdType.MESH
BF = jnp.bfloat16
F32 = jnp.float32


def mm(left, right):
    return lax.dot_general(
        left, right, (((1,), (0,)), ((), ())), preferred_element_type=F32
    )


def mm_nt(left, right):
    return lax.dot_general(
        left, right, (((1,), (1,)), ((), ())), preferred_element_type=F32
    )


def mm_tn(left, right):
    return lax.dot_general(
        left, right, (((0,), (0,)), ((), ())), preferred_element_type=F32
    )


def eye_mask(n):
    rows = lax.broadcasted_iota(jnp.int32, (n, n), 0)
    cols = lax.broadcasted_iota(jnp.int32, (n, n), 1)
    return rows == cols


def col_to_row(col):
    n = col.shape[0]
    return jnp.sum(
        jnp.where(eye_mask(n), jnp.broadcast_to(col, (n, n)), 0.0), axis=0, keepdims=True
    )


def row_to_col(row):
    n = row.shape[1]
    return jnp.sum(
        jnp.where(eye_mask(n), jnp.broadcast_to(row, (n, n)), 0.0), axis=1, keepdims=True
    )


def kernel(dims, spec, *refs):
    NE, NY, NZ, CAP, FS, T, A, H, D = dims
    NX = NE // 2
    S = NE * CAP
    SZ = S // NZ
    HC = H // 2
    HY = HC // NY
    TH = T // 2
    SH = S // 2
    RA = 32
    RB = FS - RA
    BL = NZ * 2 * FS
    R = Refs(spec, refs)

    ep = lax.axis_index("ep")
    tp = lax.axis_index("tp")
    y = tp // (NZ * 2)
    c = tp % (NZ * 2)
    z = c // 2
    k = c % 2
    x = ep // 2
    w = ep % 2

    def tp_of(yy, zz, kk):
        return (yy * NZ + zz) * 2 + kk

    def ep_dev(i):
        return {"ep": (ep + i) % NE, "tp": tp}

    def x_dev(i):
        return {"ep": ((x + i) % NX) * 2 + w, "tp": tp}

    def y_dev(i):
        return {"ep": ep, "tp": tp_of((y + i) % NY, z, k)}

    def z_dev(i):
        return {"ep": ep, "tp": tp_of(y, (z + i) % NZ, k)}

    w_dev = {"ep": x * 2 + 1 - w, "tp": tp}
    sib = {"ep": ep, "tp": tp_of(y, z, 1 - k)}
    cross = {"ep": y, "tp": tp_of(ep, z, k)}
    diag = ep == y
    off_diag = jnp.logical_not(diag)

    def remote(src, dst, sems, i, dev):
        return pltpu.make_async_remote_copy(
            src_ref=src,
            dst_ref=dst,
            send_sem=sems.at[0, i],
            recv_sem=sems.at[1, i],
            device_id=dev,
            device_id_type=MESH,
        )

    started = []

    def go(copies):
        for one in copies:
            one.start()
        started.extend(copies)
        return copies

    def arrive(copies):
        for one in copies:
            one.wait_recv()

    def to_y(ref, sems, base=0):
        return go([remote(ref, ref, sems, base + i, y_dev(i)) for i in range(1, NY)])

    def to_z(ref, sems, base=0):
        return go([remote(ref, ref, sems, base + i, z_dev(i)) for i in range(1, NZ)])

    def load(name, dst):
        one = pltpu.make_async_copy(R[name], dst, R.sem_in.at[loads[name]])
        one.start()
        return one

    names = ("table", "count", "gate", "res", "og", "gain", "wg", "wu", "wd", "ctx", "wo")
    loads = {name: i for i, name in enumerate(names)}
    own_cs = R.cs_all.at[x, w]
    ld = {}
    for name in names:
        dst = own_cs.at[pl.ds(0, A)] if name == "ctx" else R[name + "_v"]
        ld[name] = load(name, dst)

    barrier = pltpu.get_barrier_semaphore()
    for i in range(1, NE):
        pl.semaphore_signal(barrier, inc=1, device_id=ep_dev(i), device_id_type=MESH)
    for i in range(1, NY):
        pl.semaphore_signal(barrier, inc=1, device_id=y_dev(i), device_id_type=MESH)
    for i in range(1, NZ):
        pl.semaphore_signal(barrier, inc=1, device_id=z_dev(i), device_id_type=MESH)
    pl.semaphore_signal(barrier, inc=1, device_id=sib, device_id_type=MESH)

    @pl.when(off_diag)
    def _():
        pl.semaphore_signal(barrier, inc=1, device_id=cross, device_id_type=MESH)

    for name in ("table", "count", "gate"):
        ld[name].wait()
    capacity = lax.broadcasted_iota(jnp.int32, (NE, CAP), 1)
    counts = R.count_v[...]
    eyes = lax.broadcasted_iota(jnp.int32, (NE, NE), 0) == lax.broadcasted_iota(
        jnp.int32, (NE, NE), 1
    )
    count_col = jnp.sum(
        jnp.where(eyes, jnp.broadcast_to(counts, (NE, NE)), 0), axis=1, keepdims=True
    )
    table = jnp.where(capacity < count_col, R.table_v[...], -1)

    def spread(values, reps):
        rows = jnp.broadcast_to(values[:, None, :], (NE, reps * CAP, CAP)).reshape(
            NE * reps * CAP, CAP
        )
        row_id = lax.broadcasted_iota(jnp.int32, (NE * reps * CAP, CAP), 0)
        col_id = lax.broadcasted_iota(jnp.int32, (NE * reps * CAP, CAP), 1)
        hit = (row_id % CAP) == col_id
        return jnp.sum(jnp.where(hit, rows, jnp.zeros_like(rows)), axis=1, keepdims=True)

    def one_hot(column):
        lanes = lax.broadcasted_iota(jnp.int32, (column.shape[0], T), 1)
        return jnp.where(column == lanes, 1.0, 0.0).astype(BF)

    is_x = (lax.broadcasted_iota(jnp.int32, (2 * S, 1), 0) // CAP) % 2 == 0
    tokens = spread(table, 2)
    oh_x = one_hot(jnp.where(is_x, tokens, -1))
    oh_go = one_hot(jnp.where(is_x, -1, tokens))
    oh_slot = one_hot(spread(table, 1))
    scale = jnp.where(is_x, 1.0, spread(R.gate_v[...], 2))
    ld["res"].wait()
    ld["og"].wait()
    picked = mm_nt(oh_x, R.res_v[...]) + mm_nt(oh_go, R.og_v[...])
    R.a_send[...] = (scale * picked).astype(BF).reshape(NE, 2 * CAP, FS)

    peers = NE - 1 + NY - 1 + NZ
    pl.semaphore_wait(barrier, jnp.where(diag, peers, peers + 1))

    a_copies = go(
        [
            remote(R.a_send.at[(ep + i) % NE], R.a_recv.at[ep], R.sem_a, i, ep_dev(i))
            for i in range(1, NE)
        ]
    )
    og_cross = remote(R.og_v, R.og_all.at[ep, z, k], R.sem_ogt, 0, cross)

    @pl.when(off_diag)
    def _():
        og_cross.start()

    @pl.when(diag)
    def _():
        R.og_all[ep, z, k] = R.og_v[...]

    R.a_recv[ep] = R.a_send[ep]
    ld["ctx"].wait()
    R.cs_all[x, w, pl.ds(A, S)] = mm_nt(oh_slot, R.cs_all[x, w, pl.ds(0, A)]).astype(BF)
    cs1 = go([remote(own_cs, own_cs, R.sem_cs, 0, w_dev)])
    ld["wo"].wait()
    R.wo_t[...] = R.wo_v[...].T

    for name in ("gain", "wg", "wu", "wd"):
        ld[name].wait()
    arrive(a_copies)
    rows = R.a_recv[...].astype(F32).reshape(NE, 2, CAP, FS)
    rows_x = rows[:, 0].reshape(S, FS)
    rows_go = rows[:, 1].reshape(S, FS)
    gain = R.gain_v[...]
    rows_xg = (rows_x * gain).astype(BF)
    rows_gob = rows_go.astype(BF)
    other = pl.ds(pl.multiple_of((1 - k) * HC, HC), HC)
    own = pl.ds(pl.multiple_of(k * HC, HC), HC)
    lefts = (rows_xg, rows_xg, rows_gob)
    weights = (R.wg_v, R.wu_v, R.wd_v)
    for n in range(3):
        R.part_out[n] = mm(lefts[n], weights[n][:, other]).astype(BF)
    core_copies = go([remote(R.part_out, R.core_recv, R.sem_core, 0, sib)])
    sq_row = col_to_row(jnp.sum(rows_x * rows_x, axis=1, keepdims=True))
    R.tile_sq[0] = jnp.broadcast_to(sq_row, (8, S))
    sqc = go([remote(R.tile_sq.at[0], R.tile_sq_c, R.sem_sqc, 0, sib)])
    for n in range(3):
        R.part_own[n] = mm(lefts[n], weights[n][:, own])

    arrive(core_copies)
    R.part1[...] = (R.part_own[...] + R.core_recv[...].astype(F32)).astype(BF)

    def y_cols(i):
        return pl.ds(pl.multiple_of(((y + i) % NY) * HY, HY), HY)

    def z_rows(i):
        return pl.ds(pl.multiple_of(((z + i) % NZ) * SZ, SZ), SZ)

    zb = go(
        [
            remote(R.part1.at[2, z_rows(i), :], R.zb_recv.at[i - 1], R.sem_zb, i, z_dev(i))
            for i in range(1, NZ)
        ]
    )
    ya = go(
        [
            remote(
                R.part1.at[pl.ds(0, 2), :, y_cols(i)], R.ya_recv.at[i - 1], R.sem_ya, i, y_dev(i)
            )
            for i in range(1, NY)
        ]
    )
    arrive(sqc)
    R.tile_sq[1] = R.tile_sq[0] + R.tile_sq_c[...]
    sqy = go(
        [
            remote(R.tile_sq.at[1], R.tile_sq_y.at[i - 1], R.sem_sqy, i, y_dev(i))
            for i in range(1, NY)
        ]
    )

    @pl.when(off_diag)
    def _():
        og_cross.wait_recv()

    oga1 = to_y(R.og_all.at[y, z, k, pl.ds(0, RA)], R.sem_oga)
    ogb1 = to_z(R.og_all.at[y, z, k, pl.ds(RA, RB)], R.sem_ogb)
    arrive(cs1)
    cs2 = go(
        [remote(R.cs_all.at[x], R.cs_all.at[x], R.sem_cs, i, x_dev(i)) for i in range(1, NX)]
    )

    arrive(zb)
    total = R.part1[2, z_rows(0), :].astype(F32)
    for i in range(1, NZ):
        total = total + R.zb_recv[i - 1].astype(F32)
    R.part2b[...] = total.astype(BF)
    yb = go(
        [
            remote(R.part2b.at[:, y_cols(i)], R.yb_recv.at[i - 1], R.sem_yb, i, y_dev(i))
            for i in range(1, NY)
        ]
    )
    arrive(ya)
    total = R.part1[0:2, :, y_cols(0)].astype(F32)
    for i in range(1, NY):
        total = total + R.ya_recv[i - 1].astype(F32)
    R.part2[...] = total.astype(BF)
    za = go(
        [
            remote(R.part2.at[:, z_rows(i), :], R.za_recv.at[i - 1], R.sem_za, i, z_dev(i))
            for i in range(1, NZ)
        ]
    )
    arrive(sqy)
    sq = R.tile_sq[1]
    for i in range(1, NY):
        sq = sq + R.tile_sq_y[i - 1]
    R.tile_sq[2] = sq
    sqz = go(
        [
            remote(R.tile_sq.at[2], R.tile_sq_z.at[i - 1], R.sem_sqz, i, z_dev(i))
            for i in range(1, NZ)
        ]
    )

    def ring(step):
        half = step == NY // 2
        back = step - 1
        left = R.og_all.at[(y + NY - back) % NY, :, k, pl.ds(RA, RB)]
        right = R.og_all.at[(y + back) % NY, :, k, pl.ds(RA, RB)]
        if half:
            left = R.og_all.at[(y + NY - back) % NY, :, k, pl.ds(RA, RB), pl.ds(0, TH)]
            right = R.og_all.at[(y + back) % NY, :, k, pl.ds(RA, RB), pl.ds(TH, TH)]
        return go(
            [
                remote(left, left, R.sem_ring, 2 * step, y_dev(1)),
                remote(right, right, R.sem_ring, 2 * step + 1, y_dev(NY - 1)),
            ]
        )

    arrive(ogb1)
    hop = ring(1)

    arrive(sqz)
    sq = R.tile_sq[2]
    for i in range(1, NZ):
        sq = sq + R.tile_sq_z[i - 1]
    inv_col = row_to_col(lax.rsqrt(sq[0:1] / D + norm_eps))
    R.inv_buf[...] = jnp.broadcast_to(inv_col, (S, HY))
    arrive(yb)
    hid_grad = R.part2b[:, y_cols(0)].astype(F32)
    for i in range(1, NY):
        hid_grad = hid_grad + R.yb_recv[i - 1].astype(F32)
    arrive(za)
    total = R.part2[:, z_rows(0), :].astype(F32)
    for i in range(1, NZ):
        total = total + R.za_recv[i - 1].astype(F32)
    inv_mine = R.inv_buf[z_rows(0), :]
    pre_gate = inv_mine * total[0]
    pre_up = inv_mine * total[1]
    sigmoid_gate = jax.nn.sigmoid(pre_gate)
    silu_gate = pre_gate * sigmoid_gate
    hidden = (silu_gate * pre_up).astype(BF)
    d_gate = (hid_grad * pre_up * sigmoid_gate * (1.0 + pre_gate * (1.0 - sigmoid_gate))).astype(BF)
    d_up = (hid_grad * silu_gate).astype(BF)
    my_cols = pl.ds(pl.multiple_of(k * HC + y * HY, HY), HY)
    R.act[0, z_rows(0), my_cols] = d_gate
    R.act[1, z_rows(0), my_cols] = d_up
    R.act[2, z_rows(0), my_cols] = hidden

    g1 = to_z(R.act.at[0, z_rows(0), my_cols], R.sem_g1)
    u1 = to_y(R.act.at[1, z_rows(0), my_cols], R.sem_u1)
    h1 = to_z(R.act.at[2, z_rows(0), my_cols], R.sem_h1)
    dots = jnp.sum(d_gate.astype(F32) * pre_gate + d_up.astype(F32) * pre_up, axis=1, keepdims=True)
    R.dot_buf[...] = jnp.zeros_like(R.dot_buf)
    R.dot_buf[z_rows(0), :] = jnp.broadcast_to(dots, (SZ, 128))
    R.tile_dot[0] = jnp.broadcast_to(col_to_row(R.dot_buf[:, 0:1]), (8, S))
    dtz = go(
        [
            remote(R.tile_dot.at[0], R.tile_dot_z.at[i - 1], R.sem_dtz, i, z_dev(i))
            for i in range(1, NZ)
        ]
    )
    arrive(g1)
    g2 = to_y(R.act.at[0, :, my_cols], R.sem_g2)
    arrive(u1)
    u2 = to_z(R.act.at[1, z_rows(0), own], R.sem_u2)
    arrive(dtz)
    dt = R.tile_dot[0]
    for i in range(1, NZ):
        dt = dt + R.tile_dot_z[i - 1]
    R.tile_dot[1] = dt
    dty = go(
        [
            remote(R.tile_dot.at[1], R.tile_dot_y.at[i - 1], R.sem_dty, i, y_dev(i))
            for i in range(1, NY)
        ]
    )
    arrive(oga1)
    oga2 = to_z(R.og_all.at[:, z, k, pl.ds(0, RA)], R.sem_oga, NY)
    steps = NY // 2
    if steps >= 2:
        arrive(hop)
        hop = ring(2)

    arrive(g2)
    arrive(u2)
    own_act = R.act.at[pl.ds(0, 2), :, own]
    gk = go([remote(own_act, own_act, R.sem_gk, 0, sib)])
    arrive(h1)
    h2 = to_y(R.act.at[2, :, my_cols], R.sem_h2)
    arrive(dty)
    dt = R.tile_dot[1]
    for i in range(1, NY):
        dt = dt + R.tile_dot_y[i - 1]
    R.tile_dot[2] = dt
    dtc = go([remote(R.tile_dot.at[2], R.tile_dot_c, R.sem_dtc, 0, sib)])
    inv_col = R.inv_buf[:, 0:1]
    normed = rows_x * inv_col
    arrive(dtc)
    dots_col = row_to_col((R.tile_dot[2] + R.tile_dot_c[...])[0:1])
    arrive(gk)
    slot_back = (
        (mm_nt(R.act[0], R.wg_v[...]) + mm_nt(R.act[1], R.wu_v[...])).astype(BF).astype(F32)
    )
    delta = inv_col * (gain * slot_back - normed * (dots_col / D))
    R.delta_own[...] = delta.astype(BF)

    d_cross = remote(R.delta_own, R.delta_all.at[z, k, ep], R.sem_dt, 0, cross)

    @pl.when(off_diag)
    def _():
        d_cross.start()

    @pl.when(diag)
    def _():
        R.delta_all[z, k, ep] = R.delta_own[...]

    R.ret_send[...] = delta.reshape(NE, CAP, FS)
    R.ret_recv[ep] = R.ret_send[ep]
    ret_copies = go(
        [
            remote(R.ret_send.at[(ep + i) % NE], R.ret_recv.at[ep], R.sem_ret, i, ep_dev(i))
            for i in range(1, NE)
        ]
    )
    if steps >= 3:
        arrive(hop)
        hop = ring(3)
    slot_in = (normed * gain).astype(BF)
    R.gate_out[...] = mm_tn(slot_in, R.act[0]).astype(BF)

    @pl.when(off_diag)
    def _():
        d_cross.wait_recv()

    da1 = to_y(R.delta_all.at[z, k, y, pl.ds(0, SH)], R.sem_da)
    db1 = to_z(R.delta_all.at[z, k, y, pl.ds(SH, SH)], R.sem_db)
    arrive(h2)
    own_hid = R.act.at[2, :, own]
    hk = go([remote(own_hid, own_hid, R.sem_gk, 1, sib)])
    if steps >= 4:
        arrive(hop)
        hop = ring(4)
    R.up_out[...] = mm_tn(slot_in, R.act[1]).astype(BF)
    arrive(db1)
    db2 = to_y(R.delta_all.at[:, k, y, pl.ds(SH, SH)], R.sem_db, NZ)
    arrive(da1)
    da2 = to_z(R.delta_all.at[z, k, :, pl.ds(0, SH)], R.sem_da, NY)

    arrive(hop)
    arrive(oga2)
    ogk_mine = R.og_all.at[:, :, k]
    ogk = go([remote(ogk_mine, ogk_mine, R.sem_ogk, 0, sib)])
    arrive(hk)
    R.down_out[...] = mm_tn(rows_gob, R.act[2]).astype(BF)
    arrive(ogk)
    for g in range(NE):
        block = R.og_all[g].reshape(BL, T)
        R.base_send[g // 2, g % 2] = mm(R.wo_t[...], block).astype(BF)
    bx = go(
        [
            remote(R.base_send.at[(x + i) % NX], R.bx_recv.at[i - 1], R.sem_bx, i, x_dev(i))
            for i in range(1, NX)
        ]
    )
    arrive(da2)
    arrive(db2)
    dk_mine = R.delta_all.at[:, k]
    dk = go([remote(dk_mine, dk_mine, R.sem_dk, 0, sib)])
    arrive(cs2)
    for g in range(NE):
        one = mm_nt(R.og_all[g].reshape(BL, T), R.cs_all[g // 2, g % 2, pl.ds(0, A)])
        if g == 0:
            R.wo_acc[...] = one
        else:
            R.wo_acc[...] += one
    sel = R.cs_all[:, :, pl.ds(A, S)].astype(F32).reshape(NE, NE, CAP, A)
    for e in range(NE):
        R.sel_perm[e] = sel[:, e].reshape(S, A).astype(BF)

    arrive(dk)
    slots = None
    for q in range(NZ * 2):
        block = R.delta_all[q // 2, q % 2].reshape(NE * S, FS)
        one = mm(block, R.wo_v[pl.ds(q * FS, FS), :])
        slots = one if slots is None else slots + one
    slots = slots.reshape(NE, NE, CAP, A)
    for g in range(NE):
        R.msg_send[g] = slots[:, g].reshape(S, A).astype(BF)
    msg_copies = go(
        [
            remote(R.msg_send.at[(ep + i) % NE], R.msg_recv.at[ep], R.sem_msg, i, ep_dev(i))
            for i in range(1, NE)
        ]
    )
    R.msg_recv[ep] = R.msg_send[ep]
    arrive(bx)
    total = R.base_send[x].astype(F32)
    for i in range(1, NX):
        total = total + R.bx_recv[i - 1].astype(F32)
    R.base_two[...] = total.astype(BF)
    bw = go([remote(R.base_two.at[1 - w], R.bw_recv, R.sem_bx, 0, w_dev)])
    right = R.sel_perm[...].reshape(NE * S, A)
    for q in range(NZ * 2):
        feats = pl.ds(q * FS, FS)
        block = R.delta_all[q // 2, q % 2].reshape(NE * S, FS)
        R.wo_out[feats, :] = (R.wo_acc[feats, :] + mm_tn(block, right)).astype(BF)

    arrive(ret_copies)
    returned = R.ret_recv[...].reshape(S, FS).astype(BF)
    R.resid_out[...] = (R.og_v[...].astype(F32) + mm_tn(returned, oh_slot)).astype(BF)

    arrive(msg_copies)
    picked = R.msg_recv[0].astype(F32)
    for i in range(1, NE):
        picked = picked + R.msg_recv[i].astype(F32)
    slot_part = mm_tn(picked.astype(BF), oh_slot)
    arrive(bw)
    total = R.base_two[w].astype(F32) + R.bw_recv[...].astype(F32)
    R.ctx_out[...] = (total + slot_part).astype(BF)

    for one in started:
        one.wait_send()

    @pl.when(off_diag)
    def _():
        og_cross.wait_send()
        d_cross.wait_send()


class Refs:
    def __init__(self, names, refs):
        self.refs = dict(zip(names, refs, strict=True))

    def __getattr__(self, name):
        return self.refs[name]

    def __getitem__(self, name):
        return self.refs[name]


def copy_out(*refs):
    half = (len(refs) - 1) // 2
    sems = refs[-1]
    copies = [
        pltpu.make_async_copy(refs[i], refs[half + i], sems.at[i]) for i in range(half)
    ]
    for one in copies:
        one.start()
    for one in copies:
        one.wait()


def shards(
    dims,
    residual,
    out_grad,
    norm_gain,
    context,
    w_out,
    w_gate,
    w_up,
    w_down,
    slot_token,
    slot_count,
    slot_gate,
):
    NE, NY, NZ, CAP, FS, T, A, H, D = dims
    NX = NE // 2
    S = NE * CAP
    BL = NZ * 2 * FS
    HC = H // 2
    HY = HC // NY
    SZ = S // NZ
    V = pltpu.VMEM
    dma = pltpu.SemaphoreType.DMA
    hbm = pl.BlockSpec(memory_space=pltpu.HBM)
    vmem = pl.BlockSpec(memory_space=pltpu.VMEM)
    inputs = dict(
        table=slot_token[0],
        count=slot_count,
        gate=slot_gate[0],
        res=residual[0],
        og=out_grad[0],
        gain=norm_gain.reshape(1, FS),
        ctx=context[0],
        wo=w_out,
        wg=w_gate[0],
        wu=w_up[0],
        wd=w_down[0],
    )
    outs = dict(
        resid_out=(FS, T),
        ctx_out=(A, T),
        wo_out=(BL, A),
        gate_out=(FS, H),
        up_out=(FS, H),
        down_out=(FS, H),
    )
    scratch = dict(
        table_v=V((NE, CAP), jnp.int32),
        count_v=V((1, NE), jnp.int32),
        gate_v=V((NE, CAP), F32),
        res_v=V((FS, T), BF),
        og_v=V((FS, T), BF),
        gain_v=V((1, FS), F32),
        wo_v=V((BL, A), BF),
        wo_t=V((A, BL), BF),
        wg_v=V((FS, H), BF),
        wu_v=V((FS, H), BF),
        wd_v=V((FS, H), BF),
        a_send=V((NE, 2 * CAP, FS), BF),
        a_recv=V((NE, 2 * CAP, FS), BF),
        og_all=V((NE, NZ, 2, FS, T), BF),
        cs_all=V((NX, 2, A + S, T), BF),
        sel_perm=V((NE, S, A), BF),
        part_out=V((3, S, HC), BF),
        part_own=V((3, S, HC), F32),
        core_recv=V((3, S, HC), BF),
        part1=V((3, S, HC), BF),
        ya_recv=V((NY - 1, 2, S, HY), BF),
        part2=V((2, S, HY), BF),
        za_recv=V((max(NZ - 1, 1), 2, SZ, HY), BF),
        zb_recv=V((max(NZ - 1, 1), SZ, HC), BF),
        part2b=V((SZ, HC), BF),
        yb_recv=V((NY - 1, SZ, HY), BF),
        tile_sq=V((3, 8, S), F32),
        tile_sq_c=V((8, S), F32),
        tile_sq_y=V((NY - 1, 8, S), F32),
        tile_sq_z=V((max(NZ - 1, 1), 8, S), F32),
        tile_dot=V((3, 8, S), F32),
        tile_dot_c=V((8, S), F32),
        tile_dot_y=V((NY - 1, 8, S), F32),
        tile_dot_z=V((max(NZ - 1, 1), 8, S), F32),
        inv_buf=V((S, HY), F32),
        dot_buf=V((S, 128), F32),
        act=V((3, S, H), BF),
        ret_send=V((NE, CAP, FS), F32),
        ret_recv=V((NE, CAP, FS), F32),
        delta_own=V((S, FS), BF),
        delta_all=V((NZ, 2, NE, S, FS), BF),
        base_send=V((NX, 2, A, T), BF),
        bx_recv=V((max(NX - 1, 1), 2, A, T), BF),
        base_two=V((2, A, T), BF),
        bw_recv=V((A, T), BF),
        wo_acc=V((BL, A), F32),
        msg_send=V((NE, S, A), BF),
        msg_recv=V((NE, S, A), BF),
        sem_in=dma((11,)),
        sem_a=dma((2, NE)),
        sem_ogt=dma((2, 1)),
        sem_oga=dma((2, NY + NZ)),
        sem_ogb=dma((2, NZ)),
        sem_ring=dma((2, NY + 2)),
        sem_ogk=dma((2, 1)),
        sem_cs=dma((2, max(NX, 1))),
        sem_core=dma((2, 1)),
        sem_ya=dma((2, NY)),
        sem_za=dma((2, NZ)),
        sem_yb=dma((2, NY)),
        sem_zb=dma((2, NZ)),
        sem_sqc=dma((2, 1)),
        sem_sqy=dma((2, NY)),
        sem_sqz=dma((2, NZ)),
        sem_dtc=dma((2, 1)),
        sem_dty=dma((2, NY)),
        sem_dtz=dma((2, NZ)),
        sem_g1=dma((2, NZ)),
        sem_u1=dma((2, NY)),
        sem_h1=dma((2, NZ)),
        sem_g2=dma((2, NY)),
        sem_u2=dma((2, NZ)),
        sem_h2=dma((2, NY)),
        sem_gk=dma((2, 2)),
        sem_ret=dma((2, NE)),
        sem_dt=dma((2, 1)),
        sem_da=dma((2, NY + NZ)),
        sem_db=dma((2, NY + NZ)),
        sem_dk=dma((2, 1)),
        sem_bx=dma((2, max(NX, 1))),
        sem_msg=dma((2, NE)),
    )
    spec = tuple(inputs) + tuple(outs) + tuple(scratch)
    out_shape = tuple(jax.ShapeDtypeStruct(shape, BF) for shape in outs.values())
    results = pl.pallas_call(
        functools.partial(kernel, dims, spec),
        out_shape=out_shape,
        in_specs=[hbm] * len(inputs),
        out_specs=[vmem] * len(outs),
        scratch_shapes=list(scratch.values()),
        compiler_params=pltpu.CompilerParams(
            collective_id=0, has_side_effects=True, vmem_limit_bytes=48 * 1024 * 1024
        ),
    )(*inputs.values())
    resid, ctx_grad, wo_grad, gate_grad, up_grad, down_grad = pl.pallas_call(
        copy_out,
        out_shape=out_shape,
        in_specs=[vmem] * len(outs),
        out_specs=[hbm] * len(outs),
        scratch_shapes=[dma((len(outs),))],
    )(*results)
    return (
        resid[None],
        ctx_grad[None],
        wo_grad,
        gate_grad[None],
        up_grad[None],
        down_grad[None],
    )


def solution(mesh):
    sizes = dict(mesh.shape)
    NE = sizes["ep"]
    NY = NE
    NZ = sizes["tp"] // (2 * NY)

    def run(residual, out_grad, norm_gain, context, w_out, w_gate, w_up, w_down, *slots):
        D, T = residual.shape[1:]
        dims = (
            NE,
            NY,
            NZ,
            slots[0].shape[2],
            D // sizes["tp"],
            T,
            context.shape[1] // sizes["tp"],
            w_gate.shape[2],
            D,
        )
        return jax.shard_map(
            functools.partial(shards, dims),
            mesh=mesh,
            in_specs=(
                P("ep", "tp", None),
                P("ep", "tp", None),
                P("tp"),
                P("ep", "tp", None),
                P("ep", "tp"),
                P("ep", "tp", None),
                P("ep", "tp", None),
                P("ep", "tp", None),
                P("ep", None, None),
                P("ep", None),
                P("ep", None, None),
            ),
            out_specs=(
                P("ep", "tp", None),
                P("ep", "tp", None),
                P("ep", "tp"),
                P("ep", "tp", None),
                P("ep", "tp", None),
                P("ep", "tp", None),
            ),
            check_vma=False,
        )(residual, out_grad, norm_gain, context, w_out, w_gate, w_up, w_down, *slots)

    return run
```

```python
import functools

import jax
import jax.numpy as jnp
from jax import lax
from jax.experimental import pallas as pl
from jax.experimental.pallas import tpu as pltpu
from jax.sharding import PartitionSpec as P

norm_eps = 1e-06
MESH = pl.DeviceIdType.MESH
BF = jnp.bfloat16
F32 = jnp.float32


def mm(left, right):
    return lax.dot_general(
        left, right, (((1,), (0,)), ((), ())), preferred_element_type=F32
    )


def mm_nt(left, right):
    return lax.dot_general(
        left, right, (((1,), (1,)), ((), ())), preferred_element_type=F32
    )


def mm_tn(left, right):
    return lax.dot_general(
        left, right, (((0,), (0,)), ((), ())), preferred_element_type=F32
    )


def eye_mask(n):
    rows = lax.broadcasted_iota(jnp.int32, (n, n), 0)
    cols = lax.broadcasted_iota(jnp.int32, (n, n), 1)
    return rows == cols


def col_to_row(col):
    n = col.shape[0]
    return jnp.sum(
        jnp.where(eye_mask(n), jnp.broadcast_to(col, (n, n)), 0.0), axis=0, keepdims=True
    )


def row_to_col(row):
    n = row.shape[1]
    return jnp.sum(
        jnp.where(eye_mask(n), jnp.broadcast_to(row, (n, n)), 0.0), axis=1, keepdims=True
    )


def kernel(dims, spec, *refs):
    NE, NY, NZ, CAP, FS, T, A, H, D = dims
    NX = NE // 2
    S = NE * CAP
    SZ = S // NZ
    HC = H // 2
    HY = HC // NY
    TH = T // 2
    SH = S // 2
    RA = 32
    RB = FS - RA
    BL = NZ * 2 * FS
    R = Refs(spec, refs)

    ep = lax.axis_index("ep")
    tp = lax.axis_index("tp")
    y = tp // (NZ * 2)
    c = tp % (NZ * 2)
    z = c // 2
    k = c % 2
    x = ep // 2
    w = ep % 2

    def tp_of(yy, zz, kk):
        return (yy * NZ + zz) * 2 + kk

    def ep_dev(i):
        return {"ep": (ep + i) % NE, "tp": tp}

    def x_dev(i):
        return {"ep": ((x + i) % NX) * 2 + w, "tp": tp}

    def y_dev(i):
        return {"ep": ep, "tp": tp_of((y + i) % NY, z, k)}

    def z_dev(i):
        return {"ep": ep, "tp": tp_of(y, (z + i) % NZ, k)}

    w_dev = {"ep": x * 2 + 1 - w, "tp": tp}
    sib = {"ep": ep, "tp": tp_of(y, z, 1 - k)}
    cross = {"ep": y, "tp": tp_of(ep, z, k)}
    diag = ep == y
    off_diag = jnp.logical_not(diag)

    def remote(src, dst, sems, i, dev):
        return pltpu.make_async_remote_copy(
            src_ref=src,
            dst_ref=dst,
            send_sem=sems.at[0, i],
            recv_sem=sems.at[1, i],
            device_id=dev,
            device_id_type=MESH,
        )

    started = []

    def go(copies):
        for one in copies:
            one.start()
        started.extend(copies)
        return copies

    def arrive(copies):
        for one in copies:
            one.wait_recv()

    def to_y(ref, sems, base=0):
        return go([remote(ref, ref, sems, base + i, y_dev(i)) for i in range(1, NY)])

    def to_z(ref, sems, base=0):
        return go([remote(ref, ref, sems, base + i, z_dev(i)) for i in range(1, NZ)])

    def load(name, dst):
        one = pltpu.make_async_copy(R[name], dst, R.sem_in.at[loads[name]])
        one.start()
        return one

    names = ("table", "count", "gate", "res", "og", "gain", "wg", "wu", "wd", "ctx", "wo")
    loads = {name: i for i, name in enumerate(names)}
    own_cs = R.cs_all.at[x, w]
    ld = {}
    for name in names:
        dst = own_cs.at[pl.ds(0, A)] if name == "ctx" else R[name + "_v"]
        ld[name] = load(name, dst)

    outs = ("resid_out", "ctx_out", "wo_out", "gate_out", "up_out", "down_out")
    stores = []

    def store(name, value):
        R[name + "_v"][...] = value
        stored(name)

    def stored(name):
        one = pltpu.make_async_copy(R[name + "_v"], R[name], R.sem_out.at[outs.index(name)])
        one.start()
        stores.append(one)

    barrier = pltpu.get_barrier_semaphore()
    for i in range(1, NE):
        pl.semaphore_signal(barrier, inc=1, device_id=ep_dev(i), device_id_type=MESH)
    for i in range(1, NY):
        pl.semaphore_signal(barrier, inc=1, device_id=y_dev(i), device_id_type=MESH)
    for i in range(1, NZ):
        pl.semaphore_signal(barrier, inc=1, device_id=z_dev(i), device_id_type=MESH)
    pl.semaphore_signal(barrier, inc=1, device_id=sib, device_id_type=MESH)

    @pl.when(off_diag)
    def _():
        pl.semaphore_signal(barrier, inc=1, device_id=cross, device_id_type=MESH)

    for name in ("table", "count", "gate"):
        ld[name].wait()
    capacity = lax.broadcasted_iota(jnp.int32, (NE, CAP), 1)
    counts = R.count_v[...]
    eyes = lax.broadcasted_iota(jnp.int32, (NE, NE), 0) == lax.broadcasted_iota(
        jnp.int32, (NE, NE), 1
    )
    count_col = jnp.sum(
        jnp.where(eyes, jnp.broadcast_to(counts, (NE, NE)), 0), axis=1, keepdims=True
    )
    table = jnp.where(capacity < count_col, R.table_v[...], -1)

    def spread(values, reps):
        rows = jnp.broadcast_to(values[:, None, :], (NE, reps * CAP, CAP)).reshape(
            NE * reps * CAP, CAP
        )
        row_id = lax.broadcasted_iota(jnp.int32, (NE * reps * CAP, CAP), 0)
        col_id = lax.broadcasted_iota(jnp.int32, (NE * reps * CAP, CAP), 1)
        hit = (row_id % CAP) == col_id
        return jnp.sum(jnp.where(hit, rows, jnp.zeros_like(rows)), axis=1, keepdims=True)

    def one_hot(column):
        lanes = lax.broadcasted_iota(jnp.int32, (column.shape[0], T), 1)
        return jnp.where(column == lanes, 1.0, 0.0).astype(BF)

    is_x = (lax.broadcasted_iota(jnp.int32, (2 * S, 1), 0) // CAP) % 2 == 0
    tokens = spread(table, 2)
    oh_x = one_hot(jnp.where(is_x, tokens, -1))
    oh_go = one_hot(jnp.where(is_x, -1, tokens))
    oh_slot = one_hot(spread(table, 1))
    scale = jnp.where(is_x, 1.0, spread(R.gate_v[...], 2))
    ld["res"].wait()
    ld["og"].wait()
    picked = mm_nt(oh_x, R.res_v[...]) + mm_nt(oh_go, R.og_v[...])
    R.a_send[...] = (scale * picked).astype(BF).reshape(NE, 2 * CAP, FS)

    peers = NE - 1 + NY - 1 + NZ
    pl.semaphore_wait(barrier, jnp.where(diag, peers, peers + 1))

    a_copies = go(
        [
            remote(R.a_send.at[(ep + i) % NE], R.a_recv.at[ep], R.sem_a, i, ep_dev(i))
            for i in range(1, NE)
        ]
    )
    og_cross = remote(R.og_v, R.og_all.at[ep, z, k], R.sem_ogt, 0, cross)

    @pl.when(off_diag)
    def _():
        og_cross.start()

    @pl.when(diag)
    def _():
        R.og_all[ep, z, k] = R.og_v[...]

    R.a_recv[ep] = R.a_send[ep]
    ld["ctx"].wait()
    R.cs_all[x, w, pl.ds(A, S)] = mm_nt(oh_slot, R.cs_all[x, w, pl.ds(0, A)]).astype(BF)
    cs1 = go([remote(own_cs, own_cs, R.sem_cs, 0, w_dev)])
    ld["wo"].wait()
    R.wo_t[...] = R.wo_v[...].T

    for name in ("gain", "wg", "wu", "wd"):
        ld[name].wait()
    arrive(a_copies)
    rows = R.a_recv[...].astype(F32).reshape(NE, 2, CAP, FS)
    rows_x = rows[:, 0].reshape(S, FS)
    rows_go = rows[:, 1].reshape(S, FS)
    gain = R.gain_v[...]
    rows_xg = (rows_x * gain).astype(BF)
    rows_gob = rows_go.astype(BF)
    other = pl.ds(pl.multiple_of((1 - k) * HC, HC), HC)
    own = pl.ds(pl.multiple_of(k * HC, HC), HC)
    lefts = (rows_xg, rows_xg, rows_gob)
    weights = (R.wg_v, R.wu_v, R.wd_v)
    for n in range(3):
        R.part_out[n] = mm(lefts[n], weights[n][:, other]).astype(BF)
    core_copies = go([remote(R.part_out, R.core_recv, R.sem_core, 0, sib)])
    sq_row = col_to_row(jnp.sum(rows_x * rows_x, axis=1, keepdims=True))
    R.tile_sq[0] = jnp.broadcast_to(sq_row, (8, S))
    sqc = go([remote(R.tile_sq.at[0], R.tile_sq_c, R.sem_sqc, 0, sib)])
    for n in range(3):
        R.part_own[n] = mm(lefts[n], weights[n][:, own])

    arrive(core_copies)
    R.part1[...] = (R.part_own[...] + R.core_recv[...].astype(F32)).astype(BF)

    def y_cols(i):
        return pl.ds(pl.multiple_of(((y + i) % NY) * HY, HY), HY)

    def z_rows(i):
        return pl.ds(pl.multiple_of(((z + i) % NZ) * SZ, SZ), SZ)

    zb = go(
        [
            remote(R.part1.at[2, z_rows(i), :], R.zb_recv.at[i - 1], R.sem_zb, i, z_dev(i))
            for i in range(1, NZ)
        ]
    )
    ya = go(
        [
            remote(
                R.part1.at[pl.ds(0, 2), :, y_cols(i)], R.ya_recv.at[i - 1], R.sem_ya, i, y_dev(i)
            )
            for i in range(1, NY)
        ]
    )
    arrive(sqc)
    R.tile_sq[1] = R.tile_sq[0] + R.tile_sq_c[...]
    sqy = go(
        [
            remote(R.tile_sq.at[1], R.tile_sq_y.at[i - 1], R.sem_sqy, i, y_dev(i))
            for i in range(1, NY)
        ]
    )

    @pl.when(off_diag)
    def _():
        og_cross.wait_recv()

    oga1 = to_y(R.og_all.at[y, z, k, pl.ds(0, RA)], R.sem_oga)
    ogb1 = to_z(R.og_all.at[y, z, k, pl.ds(RA, RB)], R.sem_ogb)
    arrive(cs1)
    cs2 = go(
        [remote(R.cs_all.at[x], R.cs_all.at[x], R.sem_cs, i, x_dev(i)) for i in range(1, NX)]
    )

    arrive(zb)
    total = R.part1[2, z_rows(0), :].astype(F32)
    for i in range(1, NZ):
        total = total + R.zb_recv[i - 1].astype(F32)
    R.part2b[...] = total.astype(BF)
    yb = go(
        [
            remote(R.part2b.at[:, y_cols(i)], R.yb_recv.at[i - 1], R.sem_yb, i, y_dev(i))
            for i in range(1, NY)
        ]
    )
    arrive(ya)
    total = R.part1[0:2, :, y_cols(0)].astype(F32)
    for i in range(1, NY):
        total = total + R.ya_recv[i - 1].astype(F32)
    R.part2[...] = total.astype(BF)
    za = go(
        [
            remote(R.part2.at[:, z_rows(i), :], R.za_recv.at[i - 1], R.sem_za, i, z_dev(i))
            for i in range(1, NZ)
        ]
    )
    arrive(sqy)
    sq = R.tile_sq[1]
    for i in range(1, NY):
        sq = sq + R.tile_sq_y[i - 1]
    R.tile_sq[2] = sq
    sqz = go(
        [
            remote(R.tile_sq.at[2], R.tile_sq_z.at[i - 1], R.sem_sqz, i, z_dev(i))
            for i in range(1, NZ)
        ]
    )

    def ring(step):
        half = step == NY // 2
        back = step - 1
        left = R.og_all.at[(y + NY - back) % NY, :, k, pl.ds(RA, RB)]
        right = R.og_all.at[(y + back) % NY, :, k, pl.ds(RA, RB)]
        if half:
            left = R.og_all.at[(y + NY - back) % NY, :, k, pl.ds(RA, RB), pl.ds(0, TH)]
            right = R.og_all.at[(y + back) % NY, :, k, pl.ds(RA, RB), pl.ds(TH, TH)]
        return go(
            [
                remote(left, left, R.sem_ring, 2 * step, y_dev(1)),
                remote(right, right, R.sem_ring, 2 * step + 1, y_dev(NY - 1)),
            ]
        )

    arrive(ogb1)
    hop = ring(1)

    arrive(sqz)
    sq = R.tile_sq[2]
    for i in range(1, NZ):
        sq = sq + R.tile_sq_z[i - 1]
    inv_col = row_to_col(lax.rsqrt(sq[0:1] / D + norm_eps))
    R.inv_buf[...] = jnp.broadcast_to(inv_col, (S, HY))
    arrive(yb)
    hid_grad = R.part2b[:, y_cols(0)].astype(F32)
    for i in range(1, NY):
        hid_grad = hid_grad + R.yb_recv[i - 1].astype(F32)
    arrive(za)
    total = R.part2[:, z_rows(0), :].astype(F32)
    for i in range(1, NZ):
        total = total + R.za_recv[i - 1].astype(F32)
    inv_mine = R.inv_buf[z_rows(0), :]
    pre_gate = inv_mine * total[0]
    pre_up = inv_mine * total[1]
    sigmoid_gate = jax.nn.sigmoid(pre_gate)
    silu_gate = pre_gate * sigmoid_gate
    hidden = (silu_gate * pre_up).astype(BF)
    d_gate = (hid_grad * pre_up * sigmoid_gate * (1.0 + pre_gate * (1.0 - sigmoid_gate))).astype(BF)
    d_up = (hid_grad * silu_gate).astype(BF)
    my_cols = pl.ds(pl.multiple_of(k * HC + y * HY, HY), HY)
    R.act[0, z_rows(0), my_cols] = d_gate
    R.act[1, z_rows(0), my_cols] = d_up
    R.act[2, z_rows(0), my_cols] = hidden

    g1 = to_z(R.act.at[0, z_rows(0), my_cols], R.sem_g1)
    u1 = to_y(R.act.at[1, z_rows(0), my_cols], R.sem_u1)
    h1 = to_z(R.act.at[2, z_rows(0), my_cols], R.sem_h1)
    dots = jnp.sum(d_gate.astype(F32) * pre_gate + d_up.astype(F32) * pre_up, axis=1, keepdims=True)
    R.dot_buf[...] = jnp.zeros_like(R.dot_buf)
    R.dot_buf[z_rows(0), :] = jnp.broadcast_to(dots, (SZ, 128))
    R.tile_dot[0] = jnp.broadcast_to(col_to_row(R.dot_buf[:, 0:1]), (8, S))
    dtz = go(
        [
            remote(R.tile_dot.at[0], R.tile_dot_z.at[i - 1], R.sem_dtz, i, z_dev(i))
            for i in range(1, NZ)
        ]
    )
    arrive(g1)
    g2 = to_y(R.act.at[0, :, my_cols], R.sem_g2)
    arrive(u1)
    u2 = to_z(R.act.at[1, z_rows(0), own], R.sem_u2)
    arrive(dtz)
    dt = R.tile_dot[0]
    for i in range(1, NZ):
        dt = dt + R.tile_dot_z[i - 1]
    R.tile_dot[1] = dt
    dty = go(
        [
            remote(R.tile_dot.at[1], R.tile_dot_y.at[i - 1], R.sem_dty, i, y_dev(i))
            for i in range(1, NY)
        ]
    )
    arrive(oga1)
    oga2 = to_z(R.og_all.at[:, z, k, pl.ds(0, RA)], R.sem_oga, NY)
    steps = NY // 2
    if steps >= 2:
        arrive(hop)
        hop = ring(2)

    arrive(g2)
    arrive(u2)
    own_act = R.act.at[pl.ds(0, 2), :, own]
    gk = go([remote(own_act, own_act, R.sem_gk, 0, sib)])
    arrive(h1)
    h2 = to_y(R.act.at[2, :, my_cols], R.sem_h2)
    arrive(dty)
    dt = R.tile_dot[1]
    for i in range(1, NY):
        dt = dt + R.tile_dot_y[i - 1]
    R.tile_dot[2] = dt
    dtc = go([remote(R.tile_dot.at[2], R.tile_dot_c, R.sem_dtc, 0, sib)])
    inv_col = R.inv_buf[:, 0:1]
    normed = rows_x * inv_col
    arrive(dtc)
    dots_col = row_to_col((R.tile_dot[2] + R.tile_dot_c[...])[0:1])
    arrive(gk)
    slot_back = (
        (mm_nt(R.act[0], R.wg_v[...]) + mm_nt(R.act[1], R.wu_v[...])).astype(BF).astype(F32)
    )
    delta = inv_col * (gain * slot_back - normed * (dots_col / D))
    R.delta_own[...] = delta.astype(BF)

    d_cross = remote(R.delta_own, R.delta_all.at[z, k, ep], R.sem_dt, 0, cross)

    @pl.when(off_diag)
    def _():
        d_cross.start()

    @pl.when(diag)
    def _():
        R.delta_all[z, k, ep] = R.delta_own[...]

    R.ret_send[...] = delta.reshape(NE, CAP, FS)
    R.ret_recv[ep] = R.ret_send[ep]
    ret_copies = go(
        [
            remote(R.ret_send.at[(ep + i) % NE], R.ret_recv.at[ep], R.sem_ret, i, ep_dev(i))
            for i in range(1, NE)
        ]
    )
    if steps >= 3:
        arrive(hop)
        hop = ring(3)
    slot_in = (normed * gain).astype(BF)
    store("gate_out", mm_tn(slot_in, R.act[0]).astype(BF))

    @pl.when(off_diag)
    def _():
        d_cross.wait_recv()

    da1 = to_y(R.delta_all.at[z, k, y, pl.ds(0, SH)], R.sem_da)
    db1 = to_z(R.delta_all.at[z, k, y, pl.ds(SH, SH)], R.sem_db)
    arrive(h2)
    own_hid = R.act.at[2, :, own]
    hk = go([remote(own_hid, own_hid, R.sem_gk, 1, sib)])
    if steps >= 4:
        arrive(hop)
        hop = ring(4)
    store("up_out", mm_tn(slot_in, R.act[1]).astype(BF))
    arrive(db1)
    db2 = to_y(R.delta_all.at[:, k, y, pl.ds(SH, SH)], R.sem_db, NZ)
    arrive(da1)
    da2 = to_z(R.delta_all.at[z, k, :, pl.ds(0, SH)], R.sem_da, NY)

    arrive(hop)
    arrive(oga2)
    ogk_mine = R.og_all.at[:, :, k]
    ogk = go([remote(ogk_mine, ogk_mine, R.sem_ogk, 0, sib)])
    arrive(hk)
    store("down_out", mm_tn(rows_gob, R.act[2]).astype(BF))
    arrive(ogk)
    for g in range(NE):
        block = R.og_all[g].reshape(BL, T)
        R.base_send[g // 2, g % 2] = mm(R.wo_t[...], block).astype(BF)
    bx = go(
        [
            remote(R.base_send.at[(x + i) % NX], R.bx_recv.at[i - 1], R.sem_bx, i, x_dev(i))
            for i in range(1, NX)
        ]
    )
    arrive(da2)
    arrive(db2)
    dk_mine = R.delta_all.at[:, k]
    dk = go([remote(dk_mine, dk_mine, R.sem_dk, 0, sib)])
    arrive(cs2)
    for g in range(NE):
        one = mm_nt(R.og_all[g].reshape(BL, T), R.cs_all[g // 2, g % 2, pl.ds(0, A)])
        if g == 0:
            R.wo_acc[...] = one
        else:
            R.wo_acc[...] += one
    sel = R.cs_all[:, :, pl.ds(A, S)].astype(F32).reshape(NE, NE, CAP, A)
    for e in range(NE):
        R.sel_perm[e] = sel[:, e].reshape(S, A).astype(BF)

    arrive(dk)
    slots = None
    for q in range(NZ * 2):
        block = R.delta_all[q // 2, q % 2].reshape(NE * S, FS)
        one = mm(block, R.wo_v[pl.ds(q * FS, FS), :])
        slots = one if slots is None else slots + one
    slots = slots.reshape(NE, NE, CAP, A)
    for g in range(NE):
        R.msg_send[g] = slots[:, g].reshape(S, A).astype(BF)
    msg_copies = go(
        [
            remote(R.msg_send.at[(ep + i) % NE], R.msg_recv.at[ep], R.sem_msg, i, ep_dev(i))
            for i in range(1, NE)
        ]
    )
    R.msg_recv[ep] = R.msg_send[ep]
    arrive(bx)
    total = R.base_send[x].astype(F32)
    for i in range(1, NX):
        total = total + R.bx_recv[i - 1].astype(F32)
    R.base_two[...] = total.astype(BF)
    bw = go([remote(R.base_two.at[1 - w], R.bw_recv, R.sem_bx, 0, w_dev)])
    right = R.sel_perm[...].reshape(NE * S, A)
    for q in range(NZ * 2):
        feats = pl.ds(q * FS, FS)
        block = R.delta_all[q // 2, q % 2].reshape(NE * S, FS)
        R.wo_out_v[feats, :] = (R.wo_acc[feats, :] + mm_tn(block, right)).astype(BF)
    stored("wo_out")

    arrive(ret_copies)
    returned = R.ret_recv[...].reshape(S, FS).astype(BF)
    store("resid_out", (R.og_v[...].astype(F32) + mm_tn(returned, oh_slot)).astype(BF))

    arrive(msg_copies)
    picked = R.msg_recv[0].astype(F32)
    for i in range(1, NE):
        picked = picked + R.msg_recv[i].astype(F32)
    slot_part = mm_tn(picked.astype(BF), oh_slot)
    arrive(bw)
    total = R.base_two[w].astype(F32) + R.bw_recv[...].astype(F32)
    store("ctx_out", (total + slot_part).astype(BF))

    for one in started:
        one.wait_send()
    for one in stores:
        one.wait()

    @pl.when(off_diag)
    def _():
        og_cross.wait_send()
        d_cross.wait_send()


class Refs:
    def __init__(self, names, refs):
        self.refs = dict(zip(names, refs, strict=True))

    def __getattr__(self, name):
        return self.refs[name]

    def __getitem__(self, name):
        return self.refs[name]


def copy_out(*refs):
    count = (len(refs) - 1) // 3
    sources, targets, held = refs[:count], refs[count : 2 * count], refs[2 * count : -1]
    sems = refs[-1]
    loads = [
        pltpu.make_async_copy(sources[i], held[i], sems.at[0, i]) for i in range(count)
    ]
    stores = [
        pltpu.make_async_copy(held[i], targets[i], sems.at[1, i]) for i in range(count)
    ]
    for one in loads:
        one.start()
    for load, one in zip(loads, stores, strict=True):
        load.wait()
        one.start()
    for one in stores:
        one.wait()


def shards(
    dims,
    residual,
    out_grad,
    norm_gain,
    context,
    w_out,
    w_gate,
    w_up,
    w_down,
    slot_token,
    slot_count,
    slot_gate,
):
    NE, NY, NZ, CAP, FS, T, A, H, D = dims
    NX = NE // 2
    S = NE * CAP
    BL = NZ * 2 * FS
    HC = H // 2
    HY = HC // NY
    SZ = S // NZ
    V = pltpu.VMEM
    dma = pltpu.SemaphoreType.DMA
    hbm = pl.BlockSpec(memory_space=pltpu.HBM)
    inputs = dict(
        table=slot_token[0],
        count=slot_count,
        gate=slot_gate[0],
        res=residual[0],
        og=out_grad[0],
        gain=norm_gain.reshape(1, FS),
        ctx=context[0],
        wo=w_out,
        wg=w_gate[0],
        wu=w_up[0],
        wd=w_down[0],
    )
    outs = dict(
        resid_out=(FS, T),
        ctx_out=(A, T),
        wo_out=(BL, A),
        gate_out=(FS, H),
        up_out=(FS, H),
        down_out=(FS, H),
    )
    scratch = dict(
        table_v=V((NE, CAP), jnp.int32),
        count_v=V((1, NE), jnp.int32),
        gate_v=V((NE, CAP), F32),
        res_v=V((FS, T), BF),
        og_v=V((FS, T), BF),
        gain_v=V((1, FS), F32),
        wo_v=V((BL, A), BF),
        wo_t=V((A, BL), BF),
        wg_v=V((FS, H), BF),
        wu_v=V((FS, H), BF),
        wd_v=V((FS, H), BF),
        a_send=V((NE, 2 * CAP, FS), BF),
        a_recv=V((NE, 2 * CAP, FS), BF),
        og_all=V((NE, NZ, 2, FS, T), BF),
        cs_all=V((NX, 2, A + S, T), BF),
        sel_perm=V((NE, S, A), BF),
        part_out=V((3, S, HC), BF),
        part_own=V((3, S, HC), F32),
        core_recv=V((3, S, HC), BF),
        part1=V((3, S, HC), BF),
        ya_recv=V((NY - 1, 2, S, HY), BF),
        part2=V((2, S, HY), BF),
        za_recv=V((max(NZ - 1, 1), 2, SZ, HY), BF),
        zb_recv=V((max(NZ - 1, 1), SZ, HC), BF),
        part2b=V((SZ, HC), BF),
        yb_recv=V((NY - 1, SZ, HY), BF),
        tile_sq=V((3, 8, S), F32),
        tile_sq_c=V((8, S), F32),
        tile_sq_y=V((NY - 1, 8, S), F32),
        tile_sq_z=V((max(NZ - 1, 1), 8, S), F32),
        tile_dot=V((3, 8, S), F32),
        tile_dot_c=V((8, S), F32),
        tile_dot_y=V((NY - 1, 8, S), F32),
        tile_dot_z=V((max(NZ - 1, 1), 8, S), F32),
        inv_buf=V((S, HY), F32),
        dot_buf=V((S, 128), F32),
        act=V((3, S, H), BF),
        ret_send=V((NE, CAP, FS), F32),
        ret_recv=V((NE, CAP, FS), F32),
        delta_own=V((S, FS), BF),
        delta_all=V((NZ, 2, NE, S, FS), BF),
        base_send=V((NX, 2, A, T), BF),
        bx_recv=V((max(NX - 1, 1), 2, A, T), BF),
        base_two=V((2, A, T), BF),
        bw_recv=V((A, T), BF),
        wo_acc=V((BL, A), F32),
        msg_send=V((NE, S, A), BF),
        msg_recv=V((NE, S, A), BF),
        resid_out_v=V((FS, T), BF),
        ctx_out_v=V((A, T), BF),
        wo_out_v=V((BL, A), BF),
        gate_out_v=V((FS, H), BF),
        up_out_v=V((FS, H), BF),
        down_out_v=V((FS, H), BF),
        sem_in=dma((11,)),
        sem_out=dma((6,)),
        sem_a=dma((2, NE)),
        sem_ogt=dma((2, 1)),
        sem_oga=dma((2, NY + NZ)),
        sem_ogb=dma((2, NZ)),
        sem_ring=dma((2, NY + 2)),
        sem_ogk=dma((2, 1)),
        sem_cs=dma((2, max(NX, 1))),
        sem_core=dma((2, 1)),
        sem_ya=dma((2, NY)),
        sem_za=dma((2, NZ)),
        sem_yb=dma((2, NY)),
        sem_zb=dma((2, NZ)),
        sem_sqc=dma((2, 1)),
        sem_sqy=dma((2, NY)),
        sem_sqz=dma((2, NZ)),
        sem_dtc=dma((2, 1)),
        sem_dty=dma((2, NY)),
        sem_dtz=dma((2, NZ)),
        sem_g1=dma((2, NZ)),
        sem_u1=dma((2, NY)),
        sem_h1=dma((2, NZ)),
        sem_g2=dma((2, NY)),
        sem_u2=dma((2, NZ)),
        sem_h2=dma((2, NY)),
        sem_gk=dma((2, 2)),
        sem_ret=dma((2, NE)),
        sem_dt=dma((2, 1)),
        sem_da=dma((2, NY + NZ)),
        sem_db=dma((2, NY + NZ)),
        sem_dk=dma((2, 1)),
        sem_bx=dma((2, max(NX, 1))),
        sem_msg=dma((2, NE)),
    )
    spec = tuple(inputs) + tuple(outs) + tuple(scratch)
    out_shape = tuple(jax.ShapeDtypeStruct(shape, BF) for shape in outs.values())
    results = pl.pallas_call(
        functools.partial(kernel, dims, spec),
        out_shape=out_shape,
        in_specs=[hbm] * len(inputs),
        out_specs=[hbm] * len(outs),
        scratch_shapes=list(scratch.values()),
        compiler_params=pltpu.CompilerParams(
            collective_id=0, has_side_effects=True, vmem_limit_bytes=62 * 1024 * 1024
        ),
    )(*inputs.values())
    resid, ctx_grad, wo_grad, gate_grad, up_grad, down_grad = pl.pallas_call(
        copy_out,
        out_shape=out_shape,
        in_specs=[hbm] * len(outs),
        out_specs=[hbm] * len(outs),
        scratch_shapes=[V(shape, BF) for shape in outs.values()] + [dma((2, len(outs)))],
        compiler_params=pltpu.CompilerParams(vmem_limit_bytes=62 * 1024 * 1024),
    )(*results)
    return (
        resid[None],
        ctx_grad[None],
        wo_grad,
        gate_grad[None],
        up_grad[None],
        down_grad[None],
    )


def solution(mesh):
    sizes = dict(mesh.shape)
    NE = sizes["ep"]
    NY = NE
    NZ = sizes["tp"] // (2 * NY)

    def run(residual, out_grad, norm_gain, context, w_out, w_gate, w_up, w_down, *slots):
        D, T = residual.shape[1:]
        dims = (
            NE,
            NY,
            NZ,
            slots[0].shape[2],
            D // sizes["tp"],
            T,
            context.shape[1] // sizes["tp"],
            w_gate.shape[2],
            D,
        )
        return jax.shard_map(
            functools.partial(shards, dims),
            mesh=mesh,
            in_specs=(
                P("ep", "tp", None),
                P("ep", "tp", None),
                P("tp"),
                P("ep", "tp", None),
                P("ep", "tp"),
                P("ep", "tp", None),
                P("ep", "tp", None),
                P("ep", "tp", None),
                P("ep", None, None),
                P("ep", None),
                P("ep", None, None),
            ),
            out_specs=(
                P("ep", "tp", None),
                P("ep", "tp", None),
                P("ep", "tp"),
                P("ep", "tp", None),
                P("ep", "tp", None),
                P("ep", "tp", None),
            ),
            check_vma=False,
        )(residual, out_grad, norm_gain, context, w_out, w_gate, w_up, w_down, *slots)

    return run
```

```python
import functools

import jax
import jax.numpy as jnp
from jax import lax
from jax.experimental import pallas as pl
from jax.experimental.pallas import tpu as pltpu
from jax.sharding import PartitionSpec as P

norm_eps = 1e-06
MESH = pl.DeviceIdType.MESH
BF = jnp.bfloat16
F32 = jnp.float32


def mm(left, right):
    return lax.dot_general(
        left, right, (((1,), (0,)), ((), ())), preferred_element_type=F32
    )


def mm_nt(left, right):
    return lax.dot_general(
        left, right, (((1,), (1,)), ((), ())), preferred_element_type=F32
    )


def mm_tn(left, right):
    return lax.dot_general(
        left, right, (((0,), (0,)), ((), ())), preferred_element_type=F32
    )


def eye_mask(n):
    rows = lax.broadcasted_iota(jnp.int32, (n, n), 0)
    cols = lax.broadcasted_iota(jnp.int32, (n, n), 1)
    return rows == cols


def col_to_row(col):
    n = col.shape[0]
    return jnp.sum(
        jnp.where(eye_mask(n), jnp.broadcast_to(col, (n, n)), 0.0), axis=0, keepdims=True
    )


def row_to_col(row):
    n = row.shape[1]
    return jnp.sum(
        jnp.where(eye_mask(n), jnp.broadcast_to(row, (n, n)), 0.0), axis=1, keepdims=True
    )


def kernel(dims, spec, *refs):
    NE, NY, NZ, CAP, FS, T, A, H, D = dims
    NX = NE // 2
    S = NE * CAP
    SZ = S // NZ
    HC = H // 2
    HY = HC // NY
    TH = T // 2
    SH = S // 2
    BL = NZ * 2 * FS
    R = Refs(spec, refs)
    far_y = sorted(range(1, NY), key=lambda i: -min(i, NY - i))
    far_z = sorted(range(1, NZ), key=lambda i: -min(i, NZ - i))
    far_e = sorted(range(1, NE), key=lambda i: -min(i // 2, NX - i // 2))

    ep = lax.axis_index("ep")
    tp = lax.axis_index("tp")
    y = tp // (NZ * 2)
    c = tp % (NZ * 2)
    z = c // 2
    k = c % 2
    x = ep // 2
    w = ep % 2

    def tp_of(yy, zz, kk):
        return (yy * NZ + zz) * 2 + kk

    def ep_dev(i):
        return {"ep": (ep + i) % NE, "tp": tp}

    def x_dev(i):
        return {"ep": ((x + i) % NX) * 2 + w, "tp": tp}

    def y_dev(i):
        return {"ep": ep, "tp": tp_of((y + i) % NY, z, k)}

    def z_dev(i):
        return {"ep": ep, "tp": tp_of(y, (z + i) % NZ, k)}

    w_dev = {"ep": x * 2 + 1 - w, "tp": tp}
    sib = {"ep": ep, "tp": tp_of(y, z, 1 - k)}
    cross = {"ep": y, "tp": tp_of(ep, z, k)}

    diag = ep == y
    off_diag = jnp.logical_not(diag)

    def remote(src, dst, sems, i, dev):
        return pltpu.make_async_remote_copy(
            src_ref=src,
            dst_ref=dst,
            send_sem=sems.at[0, i],
            recv_sem=sems.at[1, i],
            device_id=dev,
            device_id_type=MESH,
        )

    started = []

    def go(copies):
        for one in copies:
            one.start()
        started.extend(copies)
        return copies

    def arrive(copies):
        for one in copies:
            one.wait_recv()

    def to_y(ref, sems, base=0):
        return go([remote(ref, ref, sems, base + i, y_dev(i)) for i in far_y])

    def to_z(ref, sems, base=0):
        return go([remote(ref, ref, sems, base + i, z_dev(i)) for i in far_z])

    def arrive_whole(one):
        @pl.when(off_diag)
        def _():
            one.wait_recv()

    def load(name, dst):
        one = pltpu.make_async_copy(R[name], dst, R.sem_in.at[loads[name]])
        one.start()
        return one

    names = ("table", "count", "gate", "res", "og", "gain", "wg", "wu", "wd", "ctx", "wo")
    loads = {name: i for i, name in enumerate(names)}
    own_cs = R.cs_all.at[x, w]
    ld = {}
    for name in names:
        dst = own_cs.at[pl.ds(0, A)] if name == "ctx" else R[name + "_v"]
        ld[name] = load(name, dst)

    outs = ("resid_out", "ctx_out", "wo_out", "gate_out", "up_out", "down_out")
    stores = []

    def store(name, value):
        R[name + "_v"][...] = value
        stored(name)

    def stored(name):
        one = pltpu.make_async_copy(R[name + "_v"], R[name], R.sem_out.at[outs.index(name)])
        one.start()
        stores.append(one)

    barrier = pltpu.get_barrier_semaphore()
    for i in far_e:
        pl.semaphore_signal(barrier, inc=1, device_id=ep_dev(i), device_id_type=MESH)
    for i in far_y:
        pl.semaphore_signal(barrier, inc=1, device_id=y_dev(i), device_id_type=MESH)
    for i in far_z:
        pl.semaphore_signal(barrier, inc=1, device_id=z_dev(i), device_id_type=MESH)
    pl.semaphore_signal(barrier, inc=1, device_id=sib, device_id_type=MESH)


    @pl.when(off_diag)
    def _():
        pl.semaphore_signal(barrier, inc=1, device_id=cross, device_id_type=MESH)

    for name in ("table", "count", "gate"):
        ld[name].wait()
    capacity = lax.broadcasted_iota(jnp.int32, (NE, CAP), 1)
    counts = R.count_v[...]
    eyes = lax.broadcasted_iota(jnp.int32, (NE, NE), 0) == lax.broadcasted_iota(
        jnp.int32, (NE, NE), 1
    )
    count_col = jnp.sum(
        jnp.where(eyes, jnp.broadcast_to(counts, (NE, NE)), 0), axis=1, keepdims=True
    )
    table = jnp.where(capacity < count_col, R.table_v[...], -1)

    def spread(values, reps):
        rows = jnp.broadcast_to(values[:, None, :], (NE, reps * CAP, CAP)).reshape(
            NE * reps * CAP, CAP
        )
        row_id = lax.broadcasted_iota(jnp.int32, (NE * reps * CAP, CAP), 0)
        col_id = lax.broadcasted_iota(jnp.int32, (NE * reps * CAP, CAP), 1)
        hit = (row_id % CAP) == col_id
        return jnp.sum(jnp.where(hit, rows, jnp.zeros_like(rows)), axis=1, keepdims=True)

    def one_hot(column):
        lanes = lax.broadcasted_iota(jnp.int32, (column.shape[0], T), 1)
        return jnp.where(column == lanes, 1.0, 0.0).astype(BF)

    is_x = (lax.broadcasted_iota(jnp.int32, (2 * S, 1), 0) // CAP) % 2 == 0
    tokens = spread(table, 2)
    oh_x = one_hot(jnp.where(is_x, tokens, -1))
    oh_go = one_hot(jnp.where(is_x, -1, tokens))
    oh_slot = one_hot(spread(table, 1))
    scale = jnp.where(is_x, 1.0, spread(R.gate_v[...], 2))
    ld["res"].wait()
    ld["og"].wait()
    picked = mm_nt(oh_x, R.res_v[...]) + mm_nt(oh_go, R.og_v[...])
    R.a_send[...] = (scale * picked).astype(BF).reshape(NE, 2 * CAP, FS)

    peers = NE - 1 + NY - 1 + NZ
    pl.semaphore_wait(barrier, jnp.where(diag, peers, peers + 1))

    a_copies = go(
        [
            remote(R.a_send.at[(ep + i) % NE], R.a_recv.at[ep], R.sem_a, i, ep_dev(i))
            for i in far_e
        ]
    )
    og_cross = remote(R.og_v, R.og_all.at[ep, z, k], R.sem_oga, 0, cross)

    @pl.when(off_diag)
    def _():
        og_cross.start()

    @pl.when(diag)
    def _():
        R.og_all[ep, z, k] = R.og_v[...]

    R.a_recv[ep] = R.a_send[ep]

    for name in ("gain", "wg", "wu", "wd"):
        ld[name].wait()
    arrive(a_copies)
    rows = R.a_recv[...].astype(F32).reshape(NE, 2, CAP, FS)
    arrive_whole(og_cross)
    ogb1 = to_z(R.og_all.at[y, z, k], R.sem_ogb)
    rows_x = rows[:, 0].reshape(S, FS)
    rows_go = rows[:, 1].reshape(S, FS)
    gain = R.gain_v[...]
    rows_xg = (rows_x * gain).astype(BF)
    rows_gob = rows_go.astype(BF)
    other = pl.ds(pl.multiple_of((1 - k) * HC, HC), HC)
    own = pl.ds(pl.multiple_of(k * HC, HC), HC)
    lefts = (rows_xg, rows_xg, rows_gob)
    weights = (R.wg_v, R.wu_v, R.wd_v)
    for n in range(3):
        R.part_out[n] = mm(lefts[n], weights[n][:, other]).astype(BF)
    core_copies = go([remote(R.part_out, R.core_recv, R.sem_core, 0, sib)])
    sq_row = col_to_row(jnp.sum(rows_x * rows_x, axis=1, keepdims=True))
    R.tile_sq[0] = jnp.broadcast_to(sq_row, (8, S))
    sqc = go([remote(R.tile_sq.at[0], R.tile_sq_c, R.sem_sqc, 0, sib)])
    for n in range(3):
        R.part_own[n] = mm(lefts[n], weights[n][:, own])

    arrive(core_copies)
    R.part1[...] = (R.part_own[...] + R.core_recv[...].astype(F32)).astype(BF)

    def y_cols(i):
        return pl.ds(pl.multiple_of(((y + i) % NY) * HY, HY), HY)

    def z_rows(i):
        return pl.ds(pl.multiple_of(((z + i) % NZ) * SZ, SZ), SZ)

    zb = go(
        [
            remote(R.part1.at[2, z_rows(i), :], R.zb_recv.at[i - 1], R.sem_zb, i, z_dev(i))
            for i in far_z
        ]
    )
    ya = go(
        [
            remote(
                R.part1.at[pl.ds(0, 2), :, y_cols(i)], R.ya_recv.at[i - 1], R.sem_ya, i, y_dev(i)
            )
            for i in far_y
        ]
    )
    arrive(sqc)
    R.tile_sq[1] = R.tile_sq[0] + R.tile_sq_c[...]
    sqy = go(
        [
            remote(R.tile_sq.at[1], R.tile_sq_y.at[i - 1], R.sem_sqy, i, y_dev(i))
            for i in far_y
        ]
    )

    def ring(step):
        half = step == NY // 2
        back = step - 1
        left = R.og_all.at[(y + NY - back) % NY, :, k]
        right = R.og_all.at[(y + back) % NY, :, k]
        if half:
            left = R.og_all.at[(y + NY - back) % NY, :, k, :, pl.ds(0, TH)]
            right = R.og_all.at[(y + back) % NY, :, k, :, pl.ds(TH, TH)]
        return go(
            [
                remote(left, left, R.sem_ring, 2 * step, y_dev(1)),
                remote(right, right, R.sem_ring, 2 * step + 1, y_dev(NY - 1)),
            ]
        )

    ogk = []

    def to_sib(ref):
        ogk.extend(go([remote(ref, ref, R.sem_ogk, len(ogk), sib)]))

    def hand_over(step):
        if step == NY // 2:
            to_sib(R.og_all.at[(y + step) % NY, :, k])
        else:
            to_sib(R.og_all.at[(y + step) % NY, :, k])
            to_sib(R.og_all.at[(y + NY - step) % NY, :, k])

    arrive(ogb1)
    hop = ring(1)
    to_sib(R.og_all.at[y, :, k])
    ld["ctx"].wait()
    R.cs_all[x, w, pl.ds(A, S)] = mm_nt(oh_slot, R.cs_all[x, w, pl.ds(0, A)]).astype(BF)
    cs1 = go([remote(own_cs, own_cs, R.sem_cs, 0, w_dev)])

    arrive(zb)
    total = R.part1[2, z_rows(0), :].astype(F32)
    for i in far_z:
        total = total + R.zb_recv[i - 1].astype(F32)
    R.part2b[...] = total.astype(BF)
    yb = go(
        [
            remote(R.part2b.at[:, y_cols(i)], R.yb_recv.at[i - 1], R.sem_yb, i, y_dev(i))
            for i in far_y
        ]
    )
    ld["wo"].wait()
    R.wo_t[...] = R.wo_v[...].T
    if NY // 2 >= 2:
        arrive(hop)
        hop = ring(2)
        hand_over(1)
    arrive(ya)
    total = R.part1[0:2, :, y_cols(0)].astype(F32)
    for i in far_y:
        total = total + R.ya_recv[i - 1].astype(F32)
    R.part2[...] = total.astype(BF)
    za = go(
        [
            remote(R.part2.at[:, z_rows(i), :], R.za_recv.at[i - 1], R.sem_za, i, z_dev(i))
            for i in far_z
        ]
    )
    arrive(sqy)
    sq = R.tile_sq[1]
    for i in far_y:
        sq = sq + R.tile_sq_y[i - 1]
    R.tile_sq[2] = sq
    sqz = go(
        [
            remote(R.tile_sq.at[2], R.tile_sq_z.at[i - 1], R.sem_sqz, i, z_dev(i))
            for i in far_z
        ]
    )


    arrive(cs1)
    cs2 = go(
        [remote(R.cs_all.at[x], R.cs_all.at[x], R.sem_cs, i, x_dev(i)) for i in range(1, NX)]
    )
    arrive(sqz)
    sq = R.tile_sq[2]
    for i in far_z:
        sq = sq + R.tile_sq_z[i - 1]
    inv_col = row_to_col(lax.rsqrt(sq[0:1] / D + norm_eps))
    R.inv_buf[...] = jnp.broadcast_to(inv_col, (S, HY))
    arrive(yb)
    hid_grad = R.part2b[:, y_cols(0)].astype(F32)
    for i in far_y:
        hid_grad = hid_grad + R.yb_recv[i - 1].astype(F32)
    arrive(za)
    total = R.part2[:, z_rows(0), :].astype(F32)
    for i in far_z:
        total = total + R.za_recv[i - 1].astype(F32)
    inv_mine = R.inv_buf[z_rows(0), :]
    pre_gate = inv_mine * total[0]
    pre_up = inv_mine * total[1]
    sigmoid_gate = jax.nn.sigmoid(pre_gate)
    silu_gate = pre_gate * sigmoid_gate
    hidden = (silu_gate * pre_up).astype(BF)
    d_gate = (hid_grad * pre_up * sigmoid_gate * (1.0 + pre_gate * (1.0 - sigmoid_gate))).astype(BF)
    d_up = (hid_grad * silu_gate).astype(BF)
    my_cols = pl.ds(pl.multiple_of(k * HC + y * HY, HY), HY)
    R.act[0, z_rows(0), my_cols] = d_gate
    R.act[1, z_rows(0), my_cols] = d_up
    R.act[2, z_rows(0), my_cols] = hidden

    g1 = to_z(R.act.at[0, z_rows(0), my_cols], R.sem_g1)
    u1 = to_y(R.act.at[1, z_rows(0), my_cols], R.sem_u1)
    h1 = to_z(R.act.at[2, z_rows(0), my_cols], R.sem_h1)
    dots = jnp.sum(d_gate.astype(F32) * pre_gate + d_up.astype(F32) * pre_up, axis=1, keepdims=True)
    R.dot_buf[...] = jnp.zeros_like(R.dot_buf)
    R.dot_buf[z_rows(0), :] = jnp.broadcast_to(dots, (SZ, 128))
    R.tile_dot[0] = jnp.broadcast_to(col_to_row(R.dot_buf[:, 0:1]), (8, S))
    dtz = go(
        [
            remote(R.tile_dot.at[0], R.tile_dot_z.at[i - 1], R.sem_dtz, i, z_dev(i))
            for i in far_z
        ]
    )
    if NY // 2 >= 3:
        arrive(hop)
        hop = ring(3)
        hand_over(2)
    arrive(g1)
    g2 = to_y(R.act.at[0, :, my_cols], R.sem_g2)
    arrive(u1)
    u2 = to_z(R.act.at[1, z_rows(0), own], R.sem_u2)
    arrive(dtz)
    dt = R.tile_dot[0]
    for i in far_z:
        dt = dt + R.tile_dot_z[i - 1]
    R.tile_dot[1] = dt
    dty = go(
        [
            remote(R.tile_dot.at[1], R.tile_dot_y.at[i - 1], R.sem_dty, i, y_dev(i))
            for i in far_y
        ]
    )
    if NY // 2 >= 4:
        arrive(hop)
        hop = ring(4)
        hand_over(3)

    arrive(g2)
    arrive(u2)
    own_act = R.act.at[pl.ds(0, 2), :, own]
    gk = go([remote(own_act, own_act, R.sem_gk, 0, sib)])
    arrive(dty)
    dt = R.tile_dot[1]
    for i in far_y:
        dt = dt + R.tile_dot_y[i - 1]
    R.tile_dot[2] = dt
    dtc = go([remote(R.tile_dot.at[2], R.tile_dot_c, R.sem_dtc, 0, sib)])
    inv_col = R.inv_buf[:, 0:1]
    normed = rows_x * inv_col

    def back_part(cols):
        return mm_nt(R.act[0, :, cols], R.wg_v[:, cols]) + mm_nt(R.act[1, :, cols], R.wu_v[:, cols])

    back = back_part(own)
    arrive(dtc)
    dots_col = row_to_col((R.tile_dot[2] + R.tile_dot_c[...])[0:1])
    arrive(gk)
    back = back + back_part(other)
    slot_back = back.astype(BF).astype(F32)
    delta = inv_col * (gain * slot_back - normed * (dots_col / D))
    R.delta_own[...] = delta.astype(BF)

    d_cross = remote(R.delta_own, R.delta_all.at[z, k, ep], R.sem_da, 0, cross)

    @pl.when(off_diag)
    def _():
        d_cross.start()

    @pl.when(diag)
    def _():
        R.delta_all[z, k, ep] = R.delta_own[...]

    R.ret_send[...] = delta.reshape(NE, CAP, FS)
    R.ret_recv[ep] = R.ret_send[ep]
    ret_copies = go(
        [
            remote(R.ret_send.at[(ep + i) % NE], R.ret_recv.at[ep], R.sem_ret, i, ep_dev(i))
            for i in far_e
        ]
    )
    slot_in = (normed * gain).astype(BF)
    store("gate_out", mm_tn(slot_in, R.act[0]).astype(BF))
    arrive_whole(d_cross)
    da1 = to_y(R.delta_all.at[z, k, y, pl.ds(0, SH)], R.sem_da)
    db1 = to_z(R.delta_all.at[z, k, y, pl.ds(SH, SH)], R.sem_db)
    arrive(hop)
    hand_over(NY // 2)
    store("up_out", mm_tn(slot_in, R.act[1]).astype(BF))
    arrive(db1)
    db2 = to_y(R.delta_all.at[:, k, y, pl.ds(SH, SH)], R.sem_db, NZ)
    arrive(da1)
    da2 = to_z(R.delta_all.at[z, k, :, pl.ds(0, SH)], R.sem_da, NY)
    arrive(h1)
    h2 = to_y(R.act.at[2, :, my_cols], R.sem_h2)
    arrive(ogk)

    def base(xi):
        for j in range(2):
            block = R.og_all[2 * xi + j].reshape(BL, T)
            R.base_send[xi, j] = mm(R.wo_t[...], block).astype(BF)

    bx = []
    for i in range(1, NX):
        xi = (x + i) % NX
        base(xi)
        bx += go([remote(R.base_send.at[xi], R.bx_recv.at[i - 1], R.sem_bx, i, x_dev(i))])
    base(x)
    arrive(cs2)
    for g in range(NE):
        one = mm_nt(R.og_all[g].reshape(BL, T), R.cs_all[g // 2, g % 2, pl.ds(0, A)])
        if g == 0:
            R.wo_acc[...] = one
        else:
            R.wo_acc[...] += one
    arrive(da2)
    arrive(db2)
    dk_mine = R.delta_all.at[:, k]
    dk = go([remote(dk_mine, dk_mine, R.sem_dk, 0, sib)])
    arrive(h2)
    own_hid = R.act.at[2, :, own]
    hk = go([remote(own_hid, own_hid, R.sem_gk, 1, sib)])

    def slot_part_of(kk):
        total = None
        for q in range(NZ):
            block = R.delta_all[q, kk].reshape(NE * S, FS)
            feats = pl.ds(pl.multiple_of((q * 2 + kk) * FS, 16), FS)
            one = mm(block, R.wo_v[feats, :])
            total = one if total is None else total + one
        return total

    slots = slot_part_of(k)
    arrive(dk)
    slots = slots + slot_part_of(1 - k)
    slots = slots.reshape(NE, NE, CAP, A)
    for g in range(NE):
        R.msg_send[g] = slots[:, g].reshape(S, A).astype(BF)
    msg_copies = go(
        [
            remote(R.msg_send.at[(ep + i) % NE], R.msg_recv.at[ep], R.sem_msg, i, ep_dev(i))
            for i in far_e
        ]
    )
    R.msg_recv[ep] = R.msg_send[ep]
    arrive(hk)
    store("down_out", mm_tn(rows_gob, R.act[2]).astype(BF))
    sel = R.cs_all[:, :, pl.ds(A, S)].astype(F32).reshape(NE, NE, CAP, A)
    for e in range(NE):
        R.sel_perm[e] = sel[:, e].reshape(S, A).astype(BF)
    arrive(bx)
    total = R.base_send[x].astype(F32)
    for i in range(1, NX):
        total = total + R.bx_recv[i - 1].astype(F32)
    R.base_two[...] = total.astype(BF)
    bw = go([remote(R.base_two.at[1 - w], R.bw_recv, R.sem_bx, 0, w_dev)])
    right = R.sel_perm[...].reshape(NE * S, A)
    for q in range(NZ * 2):
        feats = pl.ds(q * FS, FS)
        block = R.delta_all[q // 2, q % 2].reshape(NE * S, FS)
        R.wo_out_v[feats, :] = (R.wo_acc[feats, :] + mm_tn(block, right)).astype(BF)
    stored("wo_out")

    arrive(ret_copies)
    returned = R.ret_recv[...].reshape(S, FS).astype(BF)
    store("resid_out", (R.og_v[...].astype(F32) + mm_tn(returned, oh_slot)).astype(BF))

    arrive(msg_copies)
    picked = R.msg_recv[0].astype(F32)
    for i in far_e:
        picked = picked + R.msg_recv[i].astype(F32)
    slot_part = mm_tn(picked.astype(BF), oh_slot)
    arrive(bw)
    total = R.base_two[w].astype(F32) + R.bw_recv[...].astype(F32)
    store("ctx_out", (total + slot_part).astype(BF))

    for one in started:
        one.wait_send()
    for one in stores:
        one.wait()

    @pl.when(off_diag)
    def _():
        og_cross.wait_send()
        d_cross.wait_send()


class Refs:
    def __init__(self, names, refs):
        self.refs = dict(zip(names, refs, strict=True))

    def __getattr__(self, name):
        return self.refs[name]

    def __getitem__(self, name):
        return self.refs[name]


def copy_out(*refs):
    count = (len(refs) - 1) // 3
    sources, targets, held = refs[:count], refs[count : 2 * count], refs[2 * count : -1]
    sems = refs[-1]
    loads = [
        pltpu.make_async_copy(sources[i], held[i], sems.at[0, i]) for i in range(count)
    ]
    stores = [
        pltpu.make_async_copy(held[i], targets[i], sems.at[1, i]) for i in range(count)
    ]
    for one in loads:
        one.start()
    for load, one in zip(loads, stores, strict=True):
        load.wait()
        one.start()
    for one in stores:
        one.wait()


def shards(
    dims,
    residual,
    out_grad,
    norm_gain,
    context,
    w_out,
    w_gate,
    w_up,
    w_down,
    slot_token,
    slot_count,
    slot_gate,
):
    NE, NY, NZ, CAP, FS, T, A, H, D = dims
    NX = NE // 2
    S = NE * CAP
    BL = NZ * 2 * FS
    HC = H // 2
    HY = HC // NY
    SZ = S // NZ
    V = pltpu.VMEM
    dma = pltpu.SemaphoreType.DMA
    hbm = pl.BlockSpec(memory_space=pltpu.HBM)
    inputs = dict(
        table=slot_token[0],
        count=slot_count,
        gate=slot_gate[0],
        res=residual[0],
        og=out_grad[0],
        gain=norm_gain.reshape(1, FS),
        ctx=context[0],
        wo=w_out,
        wg=w_gate[0],
        wu=w_up[0],
        wd=w_down[0],
    )
    outs = dict(
        resid_out=(FS, T),
        ctx_out=(A, T),
        wo_out=(BL, A),
        gate_out=(FS, H),
        up_out=(FS, H),
        down_out=(FS, H),
    )
    scratch = dict(
        table_v=V((NE, CAP), jnp.int32),
        count_v=V((1, NE), jnp.int32),
        gate_v=V((NE, CAP), F32),
        res_v=V((FS, T), BF),
        og_v=V((FS, T), BF),
        gain_v=V((1, FS), F32),
        wo_v=V((BL, A), BF),
        wo_t=V((A, BL), BF),
        wg_v=V((FS, H), BF),
        wu_v=V((FS, H), BF),
        wd_v=V((FS, H), BF),
        a_send=V((NE, 2 * CAP, FS), BF),
        a_recv=V((NE, 2 * CAP, FS), BF),
        og_all=V((NE, NZ, 2, FS, T), BF),
        cs_all=V((NX, 2, A + S, T), BF),
        sel_perm=V((NE, S, A), BF),
        part_out=V((3, S, HC), BF),
        part_own=V((3, S, HC), F32),
        core_recv=V((3, S, HC), BF),
        part1=V((3, S, HC), BF),
        ya_recv=V((NY - 1, 2, S, HY), BF),
        part2=V((2, S, HY), BF),
        za_recv=V((max(NZ - 1, 1), 2, SZ, HY), BF),
        zb_recv=V((max(NZ - 1, 1), SZ, HC), BF),
        part2b=V((SZ, HC), BF),
        yb_recv=V((NY - 1, SZ, HY), BF),
        tile_sq=V((3, 8, S), F32),
        tile_sq_c=V((8, S), F32),
        tile_sq_y=V((NY - 1, 8, S), F32),
        tile_sq_z=V((max(NZ - 1, 1), 8, S), F32),
        tile_dot=V((3, 8, S), F32),
        tile_dot_c=V((8, S), F32),
        tile_dot_y=V((NY - 1, 8, S), F32),
        tile_dot_z=V((max(NZ - 1, 1), 8, S), F32),
        inv_buf=V((S, HY), F32),
        dot_buf=V((S, 128), F32),
        act=V((3, S, H), BF),
        ret_send=V((NE, CAP, FS), F32),
        ret_recv=V((NE, CAP, FS), F32),
        delta_own=V((S, FS), BF),
        delta_all=V((NZ, 2, NE, S, FS), BF),
        base_send=V((NX, 2, A, T), BF),
        bx_recv=V((max(NX - 1, 1), 2, A, T), BF),
        base_two=V((2, A, T), BF),
        bw_recv=V((A, T), BF),
        wo_acc=V((BL, A), F32),
        msg_send=V((NE, S, A), BF),
        msg_recv=V((NE, S, A), BF),
        resid_out_v=V((FS, T), BF),
        ctx_out_v=V((A, T), BF),
        wo_out_v=V((BL, A), BF),
        gate_out_v=V((FS, H), BF),
        up_out_v=V((FS, H), BF),
        down_out_v=V((FS, H), BF),
        sem_in=dma((11,)),
        sem_out=dma((6,)),
        sem_a=dma((2, NE)),
        sem_oga=dma((2, 1)),
        sem_ogb=dma((2, NZ)),
        sem_ring=dma((2, NY + 2)),
        sem_ogk=dma((2, NY + 2)),
        sem_cs=dma((2, max(NX, 1))),
        sem_core=dma((2, 1)),
        sem_ya=dma((2, NY)),
        sem_za=dma((2, NZ)),
        sem_yb=dma((2, NY)),
        sem_zb=dma((2, NZ)),
        sem_sqc=dma((2, 1)),
        sem_sqy=dma((2, NY)),
        sem_sqz=dma((2, NZ)),
        sem_dtc=dma((2, 1)),
        sem_dty=dma((2, NY)),
        sem_dtz=dma((2, NZ)),
        sem_g1=dma((2, NZ)),
        sem_u1=dma((2, NY)),
        sem_h1=dma((2, NZ)),
        sem_g2=dma((2, NY)),
        sem_u2=dma((2, NZ)),
        sem_h2=dma((2, NY)),
        sem_gk=dma((2, 2)),
        sem_ret=dma((2, NE)),
        sem_da=dma((2, NY + NZ)),
        sem_db=dma((2, NY + NZ)),
        sem_dk=dma((2, 1)),
        sem_bx=dma((2, max(NX, 1))),
        sem_msg=dma((2, NE)),
    )
    spec = tuple(inputs) + tuple(outs) + tuple(scratch)
    out_shape = tuple(jax.ShapeDtypeStruct(shape, BF) for shape in outs.values())
    results = pl.pallas_call(
        functools.partial(kernel, dims, spec),
        out_shape=out_shape,
        in_specs=[hbm] * len(inputs),
        out_specs=[hbm] * len(outs),
        scratch_shapes=list(scratch.values()),
        compiler_params=pltpu.CompilerParams(
            collective_id=0, has_side_effects=True, vmem_limit_bytes=62 * 1024 * 1024
        ),
    )(*inputs.values())
    resid, ctx_grad, wo_grad, gate_grad, up_grad, down_grad = pl.pallas_call(
        copy_out,
        out_shape=out_shape,
        in_specs=[hbm] * len(outs),
        out_specs=[hbm] * len(outs),
        scratch_shapes=[V(shape, BF) for shape in outs.values()] + [dma((2, len(outs)))],
        compiler_params=pltpu.CompilerParams(vmem_limit_bytes=62 * 1024 * 1024),
    )(*results)
    return (
        resid[None],
        ctx_grad[None],
        wo_grad,
        gate_grad[None],
        up_grad[None],
        down_grad[None],
    )


def solution(mesh):
    sizes = dict(mesh.shape)
    NE = sizes["ep"]
    NY = NE
    NZ = sizes["tp"] // (2 * NY)

    def run(residual, out_grad, norm_gain, context, w_out, w_gate, w_up, w_down, *slots):
        D, T = residual.shape[1:]
        dims = (
            NE,
            NY,
            NZ,
            slots[0].shape[2],
            D // sizes["tp"],
            T,
            context.shape[1] // sizes["tp"],
            w_gate.shape[2],
            D,
        )
        return jax.shard_map(
            functools.partial(shards, dims),
            mesh=mesh,
            in_specs=(
                P("ep", "tp", None),
                P("ep", "tp", None),
                P("tp"),
                P("ep", "tp", None),
                P("ep", "tp"),
                P("ep", "tp", None),
                P("ep", "tp", None),
                P("ep", "tp", None),
                P("ep", None, None),
                P("ep", None),
                P("ep", None, None),
            ),
            out_specs=(
                P("ep", "tp", None),
                P("ep", "tp", None),
                P("ep", "tp"),
                P("ep", "tp", None),
                P("ep", "tp", None),
                P("ep", "tp", None),
            ),
            check_vma=False,
        )(residual, out_grad, norm_gain, context, w_out, w_gate, w_up, w_down, *slots)

    return run
```

```python
import functools

import jax
import jax.numpy as jnp
from jax import lax
from jax.experimental import pallas as pl
from jax.experimental.pallas import tpu as pltpu
from jax.sharding import PartitionSpec as P

norm_eps = 1e-06
MESH = pl.DeviceIdType.MESH
BF = jnp.bfloat16
F32 = jnp.float32


def mm(left, right):
    return lax.dot_general(
        left, right, (((1,), (0,)), ((), ())), preferred_element_type=F32
    )


def mm_nt(left, right):
    return lax.dot_general(
        left, right, (((1,), (1,)), ((), ())), preferred_element_type=F32
    )


def mm_tn(left, right):
    return lax.dot_general(
        left, right, (((0,), (0,)), ((), ())), preferred_element_type=F32
    )


def eye_mask(n):
    rows = lax.broadcasted_iota(jnp.int32, (n, n), 0)
    cols = lax.broadcasted_iota(jnp.int32, (n, n), 1)
    return rows == cols


def col_to_row(col):
    n = col.shape[0]
    return jnp.sum(
        jnp.where(eye_mask(n), jnp.broadcast_to(col, (n, n)), 0.0), axis=0, keepdims=True
    )


def row_to_col(row):
    n = row.shape[1]
    return jnp.sum(
        jnp.where(eye_mask(n), jnp.broadcast_to(row, (n, n)), 0.0), axis=1, keepdims=True
    )


def kernel(dims, spec, *refs):
    NE, NY, NZ, CAP, FS, T, A, H, D = dims
    NX = NE // 2
    S = NE * CAP
    SZ = S // NZ
    HC = H // 2
    HY = HC // NY
    TH = T // 2
    SH = S // 2
    BL = NZ * 2 * FS
    R = Refs(spec, refs)
    far_y = sorted(range(1, NY), key=lambda i: -min(i, NY - i))
    far_z = sorted(range(1, NZ), key=lambda i: -min(i, NZ - i))
    far_e = sorted(range(1, NE), key=lambda i: -min(i // 2, NX - i // 2))

    ep = lax.axis_index("ep")
    tp = lax.axis_index("tp")
    y = tp // (NZ * 2)
    c = tp % (NZ * 2)
    z = c // 2
    k = c % 2
    x = ep // 2
    w = ep % 2

    def tp_of(yy, zz, kk):
        return (yy * NZ + zz) * 2 + kk

    def ep_dev(i):
        return {"ep": (ep + i) % NE, "tp": tp}

    def x_dev(i):
        return {"ep": ((x + i) % NX) * 2 + w, "tp": tp}

    def y_dev(i):
        return {"ep": ep, "tp": tp_of((y + i) % NY, z, k)}

    def z_dev(i):
        return {"ep": ep, "tp": tp_of(y, (z + i) % NZ, k)}

    w_dev = {"ep": x * 2 + 1 - w, "tp": tp}
    sib = {"ep": ep, "tp": tp_of(y, z, 1 - k)}
    cross = {"ep": y, "tp": tp_of(ep, z, k)}

    diag = ep == y
    off_diag = jnp.logical_not(diag)

    def remote(src, dst, sems, i, dev):
        return pltpu.make_async_remote_copy(
            src_ref=src,
            dst_ref=dst,
            send_sem=sems.at[0, i],
            recv_sem=sems.at[1, i],
            device_id=dev,
            device_id_type=MESH,
        )

    started = []

    def go(copies):
        for one in copies:
            one.start()
        started.extend(copies)
        return copies

    def arrive(copies):
        for one in copies:
            one.wait_recv()

    def to_y(ref, sems, base=0):
        return go([remote(ref, ref, sems, base + i, y_dev(i)) for i in far_y])

    def to_z(ref, sems, base=0):
        return go([remote(ref, ref, sems, base + i, z_dev(i)) for i in far_z])

    def arrive_whole(one):
        @pl.when(off_diag)
        def _():
            one.wait_recv()

    def load(name, dst):
        one = pltpu.make_async_copy(R[name], dst, R.sem_in.at[loads[name]])
        one.start()
        return one

    names = ("table", "count", "gate", "res", "og", "gain", "wg", "wu", "wd", "ctx", "wo")
    loads = {name: i for i, name in enumerate(names)}
    own_cs = R.cs_all.at[x, w]
    ld = {}
    for name in names:
        dst = own_cs.at[pl.ds(0, A)] if name == "ctx" else R[name + "_v"]
        ld[name] = load(name, dst)

    outs = ("resid_out", "ctx_out", "wo_out", "gate_out", "up_out", "down_out")
    stores = []

    def store(name, value):
        R[name + "_v"][...] = value
        stored(name)

    def stored(name):
        one = pltpu.make_async_copy(R[name + "_v"], R[name], R.sem_out.at[outs.index(name)])
        one.start()
        stores.append(one)

    barrier = pltpu.get_barrier_semaphore()
    for i in far_e:
        pl.semaphore_signal(barrier, inc=1, device_id=ep_dev(i), device_id_type=MESH)
    for i in far_y:
        pl.semaphore_signal(barrier, inc=1, device_id=y_dev(i), device_id_type=MESH)
    for i in far_z:
        pl.semaphore_signal(barrier, inc=1, device_id=z_dev(i), device_id_type=MESH)
    pl.semaphore_signal(barrier, inc=1, device_id=sib, device_id_type=MESH)


    @pl.when(off_diag)
    def _():
        pl.semaphore_signal(barrier, inc=1, device_id=cross, device_id_type=MESH)

    for name in ("table", "count", "gate"):
        ld[name].wait()
    capacity = lax.broadcasted_iota(jnp.int32, (NE, CAP), 1)
    counts = R.count_v[...]
    eyes = lax.broadcasted_iota(jnp.int32, (NE, NE), 0) == lax.broadcasted_iota(
        jnp.int32, (NE, NE), 1
    )
    count_col = jnp.sum(
        jnp.where(eyes, jnp.broadcast_to(counts, (NE, NE)), 0), axis=1, keepdims=True
    )
    table = jnp.where(capacity < count_col, R.table_v[...], -1)

    def spread(values, reps):
        rows = jnp.broadcast_to(values[:, None, :], (NE, reps * CAP, CAP)).reshape(
            NE * reps * CAP, CAP
        )
        row_id = lax.broadcasted_iota(jnp.int32, (NE * reps * CAP, CAP), 0)
        col_id = lax.broadcasted_iota(jnp.int32, (NE * reps * CAP, CAP), 1)
        hit = (row_id % CAP) == col_id
        return jnp.sum(jnp.where(hit, rows, jnp.zeros_like(rows)), axis=1, keepdims=True)

    def one_hot(column):
        lanes = lax.broadcasted_iota(jnp.int32, (column.shape[0], T), 1)
        return jnp.where(column == lanes, 1.0, 0.0).astype(BF)

    is_x = (lax.broadcasted_iota(jnp.int32, (2 * S, 1), 0) // CAP) % 2 == 0
    tokens = spread(table, 2)
    oh_x = one_hot(jnp.where(is_x, tokens, -1))
    oh_go = one_hot(jnp.where(is_x, -1, tokens))
    oh_slot = one_hot(spread(table, 1))
    scale = jnp.where(is_x, 1.0, spread(R.gate_v[...], 2))
    ld["res"].wait()
    ld["og"].wait()
    picked = mm_nt(oh_x, R.res_v[...]) + mm_nt(oh_go, R.og_v[...])
    R.a_send[...] = (scale * picked).astype(BF).reshape(NE, 2 * CAP, FS)

    peers = NE - 1 + NY - 1 + NZ
    pl.semaphore_wait(barrier, jnp.where(diag, peers, peers + 1))

    a_copies = go(
        [
            remote(R.a_send.at[(ep + i) % NE], R.a_recv.at[ep], R.sem_a, i, ep_dev(i))
            for i in far_e
        ]
    )
    og_cross = remote(R.og_v, R.og_all.at[ep, z, k], R.sem_oga, 0, cross)

    @pl.when(off_diag)
    def _():
        og_cross.start()

    @pl.when(diag)
    def _():
        R.og_all[ep, z, k] = R.og_v[...]

    R.a_recv[ep] = R.a_send[ep]

    for name in ("gain", "wg", "wu", "wd"):
        ld[name].wait()
    arrive(a_copies)
    rows = R.a_recv[...].astype(F32).reshape(NE, 2, CAP, FS)
    arrive_whole(og_cross)
    ogb1 = to_z(R.og_all.at[y, z, k], R.sem_ogb)
    rows_x = rows[:, 0].reshape(S, FS)
    rows_go = rows[:, 1].reshape(S, FS)
    gain = R.gain_v[...]
    rows_xg = (rows_x * gain).astype(BF)
    rows_gob = rows_go.astype(BF)
    other = pl.ds(pl.multiple_of((1 - k) * HC, HC), HC)
    own = pl.ds(pl.multiple_of(k * HC, HC), HC)
    lefts = (rows_xg, rows_xg, rows_gob)
    weights = (R.wg_v, R.wu_v, R.wd_v)
    for n in range(3):
        R.part_out[n] = mm(lefts[n], weights[n][:, other]).astype(BF)
    core_copies = go([remote(R.part_out, R.core_recv, R.sem_core, 0, sib)])
    sq_row = col_to_row(jnp.sum(rows_x * rows_x, axis=1, keepdims=True))
    R.tile_sq[0] = jnp.broadcast_to(sq_row, (8, S))
    sqc = go([remote(R.tile_sq.at[0], R.tile_sq_c, R.sem_sqc, 0, sib)])
    for n in range(3):
        R.part_own[n] = mm(lefts[n], weights[n][:, own])

    arrive(core_copies)
    R.part1[...] = (R.part_own[...] + R.core_recv[...].astype(F32)).astype(BF)

    def y_cols(i):
        return pl.ds(pl.multiple_of(((y + i) % NY) * HY, HY), HY)

    def z_rows(i):
        return pl.ds(pl.multiple_of(((z + i) % NZ) * SZ, SZ), SZ)

    zb = go(
        [
            remote(R.part1.at[2, z_rows(i), :], R.zb_recv.at[i - 1], R.sem_zb, i, z_dev(i))
            for i in far_z
        ]
    )
    ya = go(
        [
            remote(
                R.part1.at[pl.ds(0, 2), :, y_cols(i)], R.ya_recv.at[i - 1], R.sem_ya, i, y_dev(i)
            )
            for i in far_y
        ]
    )
    arrive(sqc)
    R.tile_sq[1] = R.tile_sq[0] + R.tile_sq_c[...]
    sqy = go(
        [
            remote(R.tile_sq.at[1], R.tile_sq_y.at[i - 1], R.sem_sqy, i, y_dev(i))
            for i in far_y
        ]
    )

    def ring(step):
        half = step == NY // 2
        back = step - 1
        left = R.og_all.at[(y + NY - back) % NY, :, k]
        right = R.og_all.at[(y + back) % NY, :, k]
        if half:
            left = R.og_all.at[(y + NY - back) % NY, :, k, :, pl.ds(0, TH)]
            right = R.og_all.at[(y + back) % NY, :, k, :, pl.ds(TH, TH)]
        return go(
            [
                remote(left, left, R.sem_ring, 2 * step, y_dev(1)),
                remote(right, right, R.sem_ring, 2 * step + 1, y_dev(NY - 1)),
            ]
        )

    ogk = []

    def to_sib(ref):
        ogk.extend(go([remote(ref, ref, R.sem_ogk, len(ogk), sib)]))

    def hand_over(step):
        if step == NY // 2:
            to_sib(R.og_all.at[(y + step) % NY, :, k])
        else:
            to_sib(R.og_all.at[(y + step) % NY, :, k])
            to_sib(R.og_all.at[(y + NY - step) % NY, :, k])

    arrive(ogb1)
    hop = ring(1)
    to_sib(R.og_all.at[y, :, k])

    arrive(zb)
    total = R.part1[2, z_rows(0), :].astype(F32)
    for i in far_z:
        total = total + R.zb_recv[i - 1].astype(F32)
    R.part2b[...] = total.astype(BF)
    yb = go(
        [
            remote(R.part2b.at[:, y_cols(i)], R.yb_recv.at[i - 1], R.sem_yb, i, y_dev(i))
            for i in far_y
        ]
    )
    ld["wo"].wait()
    R.wo_t[...] = R.wo_v[...].T
    if NY // 2 >= 2:
        arrive(hop)
        hop = ring(2)
        hand_over(1)
    arrive(ya)
    total = R.part1[0:2, :, y_cols(0)].astype(F32)
    for i in far_y:
        total = total + R.ya_recv[i - 1].astype(F32)
    R.part2[...] = total.astype(BF)
    za = go(
        [
            remote(R.part2.at[:, z_rows(i), :], R.za_recv.at[i - 1], R.sem_za, i, z_dev(i))
            for i in far_z
        ]
    )
    arrive(sqy)
    sq = R.tile_sq[1]
    for i in far_y:
        sq = sq + R.tile_sq_y[i - 1]
    R.tile_sq[2] = sq
    sqz = go(
        [
            remote(R.tile_sq.at[2], R.tile_sq_z.at[i - 1], R.sem_sqz, i, z_dev(i))
            for i in far_z
        ]
    )


    ld["ctx"].wait()
    R.cs_all[x, w, pl.ds(A, S)] = mm_nt(oh_slot, R.cs_all[x, w, pl.ds(0, A)]).astype(BF)
    cs1 = go([remote(own_cs, own_cs, R.sem_cs, 0, w_dev)])
    arrive(sqz)
    sq = R.tile_sq[2]
    for i in far_z:
        sq = sq + R.tile_sq_z[i - 1]
    inv_col = row_to_col(lax.rsqrt(sq[0:1] / D + norm_eps))
    R.inv_buf[...] = jnp.broadcast_to(inv_col, (S, HY))
    arrive(yb)
    hid_grad = R.part2b[:, y_cols(0)].astype(F32)
    for i in far_y:
        hid_grad = hid_grad + R.yb_recv[i - 1].astype(F32)
    arrive(za)
    total = R.part2[:, z_rows(0), :].astype(F32)
    for i in far_z:
        total = total + R.za_recv[i - 1].astype(F32)
    inv_mine = R.inv_buf[z_rows(0), :]
    pre_gate = inv_mine * total[0]
    pre_up = inv_mine * total[1]
    sigmoid_gate = jax.nn.sigmoid(pre_gate)
    silu_gate = pre_gate * sigmoid_gate
    hidden = (silu_gate * pre_up).astype(BF)
    d_gate = (hid_grad * pre_up * sigmoid_gate * (1.0 + pre_gate * (1.0 - sigmoid_gate))).astype(BF)
    d_up = (hid_grad * silu_gate).astype(BF)
    my_cols = pl.ds(pl.multiple_of(k * HC + y * HY, HY), HY)
    R.act[0, z_rows(0), my_cols] = d_gate
    R.act[1, z_rows(0), my_cols] = d_up
    R.act[2, z_rows(0), my_cols] = hidden

    g1 = to_z(R.act.at[0, z_rows(0), my_cols], R.sem_g1)
    u1 = to_y(R.act.at[1, z_rows(0), my_cols], R.sem_u1)
    h1 = to_z(R.act.at[2, z_rows(0), my_cols], R.sem_h1)
    dots = jnp.sum(d_gate.astype(F32) * pre_gate + d_up.astype(F32) * pre_up, axis=1, keepdims=True)
    R.dot_buf[...] = jnp.zeros_like(R.dot_buf)
    R.dot_buf[z_rows(0), :] = jnp.broadcast_to(dots, (SZ, 128))
    R.tile_dot[0] = jnp.broadcast_to(col_to_row(R.dot_buf[:, 0:1]), (8, S))
    dtz = go(
        [
            remote(R.tile_dot.at[0], R.tile_dot_z.at[i - 1], R.sem_dtz, i, z_dev(i))
            for i in far_z
        ]
    )
    if NY // 2 >= 3:
        arrive(hop)
        hop = ring(3)
        hand_over(2)
    arrive(g1)
    g2 = to_y(R.act.at[0, :, my_cols], R.sem_g2)
    arrive(u1)
    u2 = to_z(R.act.at[1, z_rows(0), own], R.sem_u2)
    arrive(dtz)
    dt = R.tile_dot[0]
    for i in far_z:
        dt = dt + R.tile_dot_z[i - 1]
    R.tile_dot[1] = dt
    dty = go(
        [
            remote(R.tile_dot.at[1], R.tile_dot_y.at[i - 1], R.sem_dty, i, y_dev(i))
            for i in far_y
        ]
    )
    if NY // 2 >= 4:
        arrive(hop)
        hop = ring(4)
        hand_over(3)

    arrive(cs1)
    cs2 = go(
        [remote(R.cs_all.at[x], R.cs_all.at[x], R.sem_cs, i, x_dev(i)) for i in range(1, NX)]
    )
    arrive(g2)
    arrive(u2)
    own_act = R.act.at[pl.ds(0, 2), :, own]
    gk = go([remote(own_act, own_act, R.sem_gk, 0, sib)])
    arrive(dty)
    dt = R.tile_dot[1]
    for i in far_y:
        dt = dt + R.tile_dot_y[i - 1]
    R.tile_dot[2] = dt
    dtc = go([remote(R.tile_dot.at[2], R.tile_dot_c, R.sem_dtc, 0, sib)])
    inv_col = R.inv_buf[:, 0:1]
    normed = rows_x * inv_col

    def back_part(cols):
        return mm_nt(R.act[0, :, cols], R.wg_v[:, cols]) + mm_nt(R.act[1, :, cols], R.wu_v[:, cols])

    back = back_part(own)
    arrive(dtc)
    dots_col = row_to_col((R.tile_dot[2] + R.tile_dot_c[...])[0:1])
    arrive(gk)
    back = back + back_part(other)
    slot_back = back.astype(BF).astype(F32)
    delta = inv_col * (gain * slot_back - normed * (dots_col / D))
    R.delta_own[...] = delta.astype(BF)

    d_cross = remote(R.delta_own, R.delta_all.at[z, k, ep], R.sem_da, 0, cross)

    @pl.when(off_diag)
    def _():
        d_cross.start()

    @pl.when(diag)
    def _():
        R.delta_all[z, k, ep] = R.delta_own[...]

    R.ret_send[...] = delta.reshape(NE, CAP, FS)
    R.ret_recv[ep] = R.ret_send[ep]
    ret_copies = go(
        [
            remote(R.ret_send.at[(ep + i) % NE], R.ret_recv.at[ep], R.sem_ret, i, ep_dev(i))
            for i in far_e
        ]
    )
    slot_in = (normed * gain).astype(BF)
    store("gate_out", mm_tn(slot_in, R.act[0]).astype(BF))
    arrive_whole(d_cross)
    da1 = to_y(R.delta_all.at[z, k, y, pl.ds(0, SH)], R.sem_da)
    db1 = to_z(R.delta_all.at[z, k, y, pl.ds(SH, SH)], R.sem_db)
    arrive(hop)
    hand_over(NY // 2)
    arrive(db1)
    db2 = to_y(R.delta_all.at[:, k, y, pl.ds(SH, SH)], R.sem_db, NZ)
    arrive(da1)
    da2 = to_z(R.delta_all.at[z, k, :, pl.ds(0, SH)], R.sem_da, NY)
    arrive(ogk)

    def base(xi):
        for j in range(2):
            block = R.og_all[2 * xi + j].reshape(BL, T)
            R.base_send[xi, j] = mm(R.wo_t[...], block).astype(BF)

    bx = []
    for i in range(1, NX):
        xi = (x + i) % NX
        base(xi)
        bx += go([remote(R.base_send.at[xi], R.bx_recv.at[i - 1], R.sem_bx, i, x_dev(i))])
    arrive(h1)
    h2 = to_y(R.act.at[2, :, my_cols], R.sem_h2)
    base(x)
    store("up_out", mm_tn(slot_in, R.act[1]).astype(BF))
    arrive(cs2)
    for g in range(NE):
        one = mm_nt(R.og_all[g].reshape(BL, T), R.cs_all[g // 2, g % 2, pl.ds(0, A)])
        if g == 0:
            R.wo_acc[...] = one
        else:
            R.wo_acc[...] += one
    arrive(da2)
    arrive(db2)
    dk_mine = R.delta_all.at[:, k]
    dk = go([remote(dk_mine, dk_mine, R.sem_dk, 0, sib)])
    arrive(h2)
    own_hid = R.act.at[2, :, own]
    hk = go([remote(own_hid, own_hid, R.sem_gk, 1, sib)])

    def slot_part_of(kk):
        total = None
        for q in range(NZ):
            block = R.delta_all[q, kk].reshape(NE * S, FS)
            feats = pl.ds(pl.multiple_of((q * 2 + kk) * FS, 16), FS)
            one = mm(block, R.wo_v[feats, :])
            total = one if total is None else total + one
        return total

    slots = slot_part_of(k)
    arrive(dk)
    slots = slots + slot_part_of(1 - k)
    slots = slots.reshape(NE, NE, CAP, A)
    for g in range(NE):
        R.msg_send[g] = slots[:, g].reshape(S, A).astype(BF)
    msg_copies = go(
        [
            remote(R.msg_send.at[(ep + i) % NE], R.msg_recv.at[ep], R.sem_msg, i, ep_dev(i))
            for i in far_e
        ]
    )
    R.msg_recv[ep] = R.msg_send[ep]
    arrive(hk)
    store("down_out", mm_tn(rows_gob, R.act[2]).astype(BF))
    sel = R.cs_all[:, :, pl.ds(A, S)].astype(F32).reshape(NE, NE, CAP, A)
    for e in range(NE):
        R.sel_perm[e] = sel[:, e].reshape(S, A).astype(BF)
    arrive(bx)
    total = R.base_send[x].astype(F32)
    for i in range(1, NX):
        total = total + R.bx_recv[i - 1].astype(F32)
    R.base_two[...] = total.astype(BF)
    bw = go([remote(R.base_two.at[1 - w], R.bw_recv, R.sem_bx, 0, w_dev)])
    right = R.sel_perm[...].reshape(NE * S, A)
    for q in range(NZ * 2):
        feats = pl.ds(q * FS, FS)
        block = R.delta_all[q // 2, q % 2].reshape(NE * S, FS)
        R.wo_out_v[feats, :] = (R.wo_acc[feats, :] + mm_tn(block, right)).astype(BF)
    stored("wo_out")

    arrive(ret_copies)
    returned = R.ret_recv[...].reshape(S, FS).astype(BF)
    store("resid_out", (R.og_v[...].astype(F32) + mm_tn(returned, oh_slot)).astype(BF))

    arrive(msg_copies)
    picked = R.msg_recv[0].astype(F32)
    for i in far_e:
        picked = picked + R.msg_recv[i].astype(F32)
    slot_part = mm_tn(picked.astype(BF), oh_slot)
    arrive(bw)
    total = R.base_two[w].astype(F32) + R.bw_recv[...].astype(F32)
    store("ctx_out", (total + slot_part).astype(BF))

    for one in started:
        one.wait_send()
    for one in stores:
        one.wait()

    @pl.when(off_diag)
    def _():
        og_cross.wait_send()
        d_cross.wait_send()


class Refs:
    def __init__(self, names, refs):
        self.refs = dict(zip(names, refs, strict=True))

    def __getattr__(self, name):
        return self.refs[name]

    def __getitem__(self, name):
        return self.refs[name]


def copy_out(*refs):
    count = (len(refs) - 1) // 3
    sources, targets, held = refs[:count], refs[count : 2 * count], refs[2 * count : -1]
    sems = refs[-1]
    loads = [
        pltpu.make_async_copy(sources[i], held[i], sems.at[0, i]) for i in range(count)
    ]
    stores = [
        pltpu.make_async_copy(held[i], targets[i], sems.at[1, i]) for i in range(count)
    ]
    for one in loads:
        one.start()
    for load, one in zip(loads, stores, strict=True):
        load.wait()
        one.start()
    for one in stores:
        one.wait()


def shards(
    dims,
    residual,
    out_grad,
    norm_gain,
    context,
    w_out,
    w_gate,
    w_up,
    w_down,
    slot_token,
    slot_count,
    slot_gate,
):
    NE, NY, NZ, CAP, FS, T, A, H, D = dims
    NX = NE // 2
    S = NE * CAP
    BL = NZ * 2 * FS
    HC = H // 2
    HY = HC // NY
    SZ = S // NZ
    V = pltpu.VMEM
    dma = pltpu.SemaphoreType.DMA
    hbm = pl.BlockSpec(memory_space=pltpu.HBM)
    inputs = dict(
        table=slot_token[0],
        count=slot_count,
        gate=slot_gate[0],
        res=residual[0],
        og=out_grad[0],
        gain=norm_gain.reshape(1, FS),
        ctx=context[0],
        wo=w_out,
        wg=w_gate[0],
        wu=w_up[0],
        wd=w_down[0],
    )
    outs = dict(
        resid_out=(FS, T),
        ctx_out=(A, T),
        wo_out=(BL, A),
        gate_out=(FS, H),
        up_out=(FS, H),
        down_out=(FS, H),
    )
    scratch = dict(
        table_v=V((NE, CAP), jnp.int32),
        count_v=V((1, NE), jnp.int32),
        gate_v=V((NE, CAP), F32),
        res_v=V((FS, T), BF),
        og_v=V((FS, T), BF),
        gain_v=V((1, FS), F32),
        wo_v=V((BL, A), BF),
        wo_t=V((A, BL), BF),
        wg_v=V((FS, H), BF),
        wu_v=V((FS, H), BF),
        wd_v=V((FS, H), BF),
        a_send=V((NE, 2 * CAP, FS), BF),
        a_recv=V((NE, 2 * CAP, FS), BF),
        og_all=V((NE, NZ, 2, FS, T), BF),
        cs_all=V((NX, 2, A + S, T), BF),
        sel_perm=V((NE, S, A), BF),
        part_out=V((3, S, HC), BF),
        part_own=V((3, S, HC), F32),
        core_recv=V((3, S, HC), BF),
        part1=V((3, S, HC), BF),
        ya_recv=V((NY - 1, 2, S, HY), BF),
        part2=V((2, S, HY), BF),
        za_recv=V((max(NZ - 1, 1), 2, SZ, HY), BF),
        zb_recv=V((max(NZ - 1, 1), SZ, HC), BF),
        part2b=V((SZ, HC), BF),
        yb_recv=V((NY - 1, SZ, HY), BF),
        tile_sq=V((3, 8, S), F32),
        tile_sq_c=V((8, S), F32),
        tile_sq_y=V((NY - 1, 8, S), F32),
        tile_sq_z=V((max(NZ - 1, 1), 8, S), F32),
        tile_dot=V((3, 8, S), F32),
        tile_dot_c=V((8, S), F32),
        tile_dot_y=V((NY - 1, 8, S), F32),
        tile_dot_z=V((max(NZ - 1, 1), 8, S), F32),
        inv_buf=V((S, HY), F32),
        dot_buf=V((S, 128), F32),
        act=V((3, S, H), BF),
        ret_send=V((NE, CAP, FS), F32),
        ret_recv=V((NE, CAP, FS), F32),
        delta_own=V((S, FS), BF),
        delta_all=V((NZ, 2, NE, S, FS), BF),
        base_send=V((NX, 2, A, T), BF),
        bx_recv=V((max(NX - 1, 1), 2, A, T), BF),
        base_two=V((2, A, T), BF),
        bw_recv=V((A, T), BF),
        wo_acc=V((BL, A), F32),
        msg_send=V((NE, S, A), BF),
        msg_recv=V((NE, S, A), BF),
        resid_out_v=V((FS, T), BF),
        ctx_out_v=V((A, T), BF),
        wo_out_v=V((BL, A), BF),
        gate_out_v=V((FS, H), BF),
        up_out_v=V((FS, H), BF),
        down_out_v=V((FS, H), BF),
        sem_in=dma((11,)),
        sem_out=dma((6,)),
        sem_a=dma((2, NE)),
        sem_oga=dma((2, 1)),
        sem_ogb=dma((2, NZ)),
        sem_ring=dma((2, NY + 2)),
        sem_ogk=dma((2, NY + 2)),
        sem_cs=dma((2, max(NX, 1))),
        sem_core=dma((2, 1)),
        sem_ya=dma((2, NY)),
        sem_za=dma((2, NZ)),
        sem_yb=dma((2, NY)),
        sem_zb=dma((2, NZ)),
        sem_sqc=dma((2, 1)),
        sem_sqy=dma((2, NY)),
        sem_sqz=dma((2, NZ)),
        sem_dtc=dma((2, 1)),
        sem_dty=dma((2, NY)),
        sem_dtz=dma((2, NZ)),
        sem_g1=dma((2, NZ)),
        sem_u1=dma((2, NY)),
        sem_h1=dma((2, NZ)),
        sem_g2=dma((2, NY)),
        sem_u2=dma((2, NZ)),
        sem_h2=dma((2, NY)),
        sem_gk=dma((2, 2)),
        sem_ret=dma((2, NE)),
        sem_da=dma((2, NY + NZ)),
        sem_db=dma((2, NY + NZ)),
        sem_dk=dma((2, 1)),
        sem_bx=dma((2, max(NX, 1))),
        sem_msg=dma((2, NE)),
    )
    spec = tuple(inputs) + tuple(outs) + tuple(scratch)
    out_shape = tuple(jax.ShapeDtypeStruct(shape, BF) for shape in outs.values())
    results = pl.pallas_call(
        functools.partial(kernel, dims, spec),
        out_shape=out_shape,
        in_specs=[hbm] * len(inputs),
        out_specs=[hbm] * len(outs),
        scratch_shapes=list(scratch.values()),
        compiler_params=pltpu.CompilerParams(
            collective_id=0, has_side_effects=True, vmem_limit_bytes=62 * 1024 * 1024
        ),
    )(*inputs.values())
    resid, ctx_grad, wo_grad, gate_grad, up_grad, down_grad = pl.pallas_call(
        copy_out,
        out_shape=out_shape,
        in_specs=[hbm] * len(outs),
        out_specs=[hbm] * len(outs),
        scratch_shapes=[V(shape, BF) for shape in outs.values()] + [dma((2, len(outs)))],
        compiler_params=pltpu.CompilerParams(vmem_limit_bytes=62 * 1024 * 1024),
    )(*results)
    return (
        resid[None],
        ctx_grad[None],
        wo_grad,
        gate_grad[None],
        up_grad[None],
        down_grad[None],
    )


def solution(mesh):
    sizes = dict(mesh.shape)
    NE = sizes["ep"]
    NY = NE
    NZ = sizes["tp"] // (2 * NY)

    def run(residual, out_grad, norm_gain, context, w_out, w_gate, w_up, w_down, *slots):
        D, T = residual.shape[1:]
        dims = (
            NE,
            NY,
            NZ,
            slots[0].shape[2],
            D // sizes["tp"],
            T,
            context.shape[1] // sizes["tp"],
            w_gate.shape[2],
            D,
        )
        return jax.shard_map(
            functools.partial(shards, dims),
            mesh=mesh,
            in_specs=(
                P("ep", "tp", None),
                P("ep", "tp", None),
                P("tp"),
                P("ep", "tp", None),
                P("ep", "tp"),
                P("ep", "tp", None),
                P("ep", "tp", None),
                P("ep", "tp", None),
                P("ep", None, None),
                P("ep", None),
                P("ep", None, None),
            ),
            out_specs=(
                P("ep", "tp", None),
                P("ep", "tp", None),
                P("ep", "tp"),
                P("ep", "tp", None),
                P("ep", "tp", None),
                P("ep", "tp", None),
            ),
            check_vma=False,
        )(residual, out_grad, norm_gain, context, w_out, w_gate, w_up, w_down, *slots)

    return run
```
